32 devices in a mesh: fsdp: 8 (over y, x, core), tensor: 4 (over z).
Axes of the slice: x: 2, y: 2, z: 4, core: 2. Of those that a mesh axis runs over, the one named last changes fastest.
Arguments:
- layer_input: bfloat16 [1, 4096, 1024], P(None, ('fsdp', 'tensor')), may hold values from -6 to 6
- out_grad: bfloat16 [1, 4096, 1024], P(None, ('fsdp', 'tensor')), may hold values from -6 to 6
- segments: int32 [1, 32, 128], P(None, 'fsdp'), may hold values from 0 to 3, as said below
- positions: int32 [1, 32, 128], P(None, 'fsdp'), may hold values from 0 to 2047, as said below
- qkv_weight: bfloat16 [1024, 3072], P('fsdp', 'tensor')
- qkv_bias: bfloat16 [16, 192], P('tensor', 'fsdp'), may hold values from -3 to 3
- dense_weight: bfloat16 [1024, 1024], P('tensor', 'fsdp'), may hold values from -1 to 1
- dense_bias: float32 [1024], P(('fsdp', 'tensor')), may hold values from -3 to 3
- inner_weight: bfloat16 [1024, 4096], P('fsdp', 'tensor'), may hold values from -0.1875 to 0.1875
- inner_bias: bfloat16 [16, 256], P('tensor', 'fsdp'), may hold values from -3 to 3
- outer_weight: bfloat16 [4096, 1024], P('tensor', 'fsdp'), may hold values from -0.09375 to 0.09375
- outer_bias: float32 [1024], P(('fsdp', 'tensor')), may hold values from -3 to 3
- attention_norm_gain: float32 [1024], P(('fsdp', 'tensor')), may hold values from 0.1 to 1.9
- attention_norm_bias: float32 [1024], P(('fsdp', 'tensor')), may hold values from -3 to 3
- feedforward_norm_gain: float32 [1024], P(('fsdp', 'tensor')), may hold values from 0.1 to 1.9
- feedforward_norm_bias: float32 [1024], P(('fsdp', 'tensor')), may hold values from -3 to 3
Outputs:
- layer_out: bfloat16 [1, 4096, 1024], P(None, ('fsdp', 'tensor'))
- in_grad: bfloat16 [1, 4096, 1024], P(None, ('fsdp', 'tensor'))
- qkv_weight_grad: float32 [1024, 3072], P('fsdp', 'tensor')
- qkv_bias_grad: float32 [16, 192], P('tensor', 'fsdp')
- dense_weight_grad: float32 [1024, 1024], P('tensor', 'fsdp')
- dense_bias_grad: float32 [1024], P(('fsdp', 'tensor'))
- inner_weight_grad: float32 [1024, 4096], P('fsdp', 'tensor')
- inner_bias_grad: float32 [16, 256], P('tensor', 'fsdp')
- outer_weight_grad: float32 [4096, 1024], P('tensor', 'fsdp')
- outer_bias_grad: float32 [1024], P(('fsdp', 'tensor'))
- norm1_gain_grad: float32 [1024], P(('fsdp', 'tensor'))
- norm1_shift_grad: float32 [1024], P(('fsdp', 'tensor'))
- norm2_gain_grad: float32 [1024], P(('fsdp', 'tensor'))
- norm2_shift_grad: float32 [1024], P(('fsdp', 'tensor'))
The draws below stay inside these ranges and needn't reach their ends.
Inputs may be any that keep to these rules, and one draw needn't show every extreme that they name: `segments`: each sequence of 128 tokens holds exactly 4 documents, numbered from 0 in order and never falling, each of one token or more. Within a document positions rise by one or two from token to token; every document but the first of a sequence starts at 0.
All inputs are finite; a program needn't handle non-finite values.
Results may differ from the reference program's by a relative error of at most 0.015.
Values may be sent and summed in bfloat16 or wider, within the bound.
No kernel may reach another device: no remote copies, remote signals or barrier semaphores. Data moves between devices by JAX's collectives and lax.ppermute only.
A program may use at most 128 MiB of HBM per device.

```python
import jax
import jax.numpy as jnp
from jax import lax

D = 1024
H = 16
HD = 64
ROT = 16
FF = 4096
LEN = 128
DOCS = 4
MB = 1
SEQ_MB = 4
SEQ_STEP = 32
TOK_STEP = 4096
N_FSDP = 8


context_limit = 2048


def document_layout(key):
    index = jnp.arange(LEN, dtype=jnp.int32)
    tie = jax.random.randint(jax.random.fold_in(key, 11), (MB, SEQ_STEP, LEN - 1), 0, 1 << 20)
    unused_result, picks = lax.top_k(tie * LEN + index[:LEN - 1], DOCS - 1)
    cuts = (picks.astype(jnp.int32) + 1)[:, :, None, :]
    after = index[None, None, :, None] >= cuts
    segment = jnp.sum(after.astype(jnp.int32), -1).astype(jnp.int32)
    start = jnp.max(jnp.where(after, cuts, 0), -1).astype(jnp.int32)
    stride = jax.random.randint(jax.random.fold_in(key, 12), (MB, SEQ_STEP, LEN), 1, 3)
    before = jnp.cumsum(stride, -1) - stride
    base = jnp.take_along_axis(before, start, -1)
    offset = jax.random.randint(jax.random.fold_in(key, 13), (MB, SEQ_STEP, 1), 0, context_limit - 2 * LEN)
    first_top = jnp.max(jnp.where(segment == 0, before, 0), -1, keepdims=True).astype(jnp.int32)
    batch_index = jnp.arange(MB, dtype=jnp.int32)[:, None, None]
    seq_index = jnp.arange(SEQ_STEP, dtype=jnp.int32)[None, :, None]
    leading = (batch_index == 0) & (seq_index == 0)
    offset = jnp.where(leading, context_limit - 1 - first_top, offset).astype(jnp.int32)
    position = before - base + jnp.where(segment == 0, offset, 0)
    return (segment.astype(jnp.int32), position.astype(jnp.int32))


def draw_segments(key, part):
    return document_layout(key)[0]


def draw_positions(key, part):
    return document_layout(key)[1]


def draw_qkv_weight(key, part):
    base = jax.random.normal(jax.random.fold_in(key, 21), (D, H, 3, HD), jnp.float32) * D ** (-0.5)
    return base.reshape(D, 3 * D).astype(jnp.bfloat16)


def shard_levels(rng, dims, cuts, least, top_value):
    loudness, own = 1.0, jax.random.fold_in(rng, 6)
    for dim, shards_of in cuts:
        draws = jnp.exp(jax.random.uniform(jax.random.fold_in(own, dim), (shards_of,), jnp.float32, least / len(cuts), top_value / len(cuts)))
        loudness = loudness * jnp.repeat(draws, dims[dim] // shards_of).reshape([-1 if axis == dim else 1 for axis in range(len(dims))])
    return loudness


def normal_values(own_key, extent, scale, reach, shards=(), kind=jnp.bfloat16):
    drawn = jax.random.normal(own_key, extent, jnp.float32) * scale
    if len(shards) > 0:
        drawn = shard_levels(own_key, extent, shards, -0.22, 0.18) * drawn
    return jnp.clip(drawn, min=-reach, max=reach).astype(kind)


def setup_inputs(seed: int = 0) -> dict:
    streams_of = jax.random.split(jax.random.key(seed), 17)
    return {
        "layer_input": normal_values(streams_of[0], (MB, TOK_STEP, D), 1.0, 6.0, ((1, 32),)),
        "out_grad": normal_values(streams_of[1], (MB, TOK_STEP, D), 1.0, 6.0, ((1, 32),)),
        "segments": draw_segments(jax.random.fold_in(streams_of[16], 71), 0),
        "positions": draw_positions(jax.random.fold_in(streams_of[16], 71), 0),
        "qkv_weight": draw_qkv_weight(jax.random.fold_in(streams_of[16], 71), 0),
        "qkv_bias": normal_values(streams_of[5], (H, 3 * HD), 0.5, 3.0, ((0, 4), (1, 8))),
        "dense_weight": normal_values(streams_of[6], (D, D), (D // 32) ** -0.5, 1.0, ((0, 4), (1, 8))),
        "dense_bias": normal_values(streams_of[7], (D,), 0.5, 3.0, ((0, 32),), jnp.float32),
        "inner_weight": normal_values(streams_of[8], (D, FF), D ** -0.5, 0.1875, ((0, 8), (1, 4))),
        "inner_bias": normal_values(streams_of[9], (H, FF // H), 0.5, 3.0, ((0, 4), (1, 8))),
        "outer_weight": normal_values(streams_of[10], (FF, D), FF ** -0.5, 0.09375, ((0, 4), (1, 8))),
        "outer_bias": normal_values(streams_of[11], (D,), 0.5, 3.0, ((0, 32),), jnp.float32),
        "attention_norm_gain": jnp.clip(1.0 + 0.18 * jax.random.normal(streams_of[12], (D,), jnp.float32), 0.1, 1.9),
        "attention_norm_bias": normal_values(streams_of[13], (D,), 0.5, 3.0, ((0, 32),), jnp.float32),
        "feedforward_norm_gain": jnp.clip(1.0 + 0.18 * jax.random.normal(streams_of[14], (D,), jnp.float32), 0.1, 1.9),
        "feedforward_norm_bias": normal_values(streams_of[15], (D,), 0.5, 3.0, ((0, 32),), jnp.float32),
    }


EPS = 1e-05
ROOT_HALF = 0.7071067811865476
INV_ROOT_TAU = 0.3989422804014327
MASKED = -1e+30

def normalize_rows(token_row_block):
    values = token_row_block.astype(jnp.float32)
    centre = values - lax.optimization_barrier(jnp.mean(values, -1, keepdims=True))
    scale = lax.rsqrt(lax.optimization_barrier(jnp.mean(centre * centre, -1, keepdims=True)) + EPS)
    return (centre * scale, scale)

def gelu_value(pre):
    return 0.5 * pre * (1.0 + lax.erf(pre * ROOT_HALF))

def gelu_slope(pre):
    return 0.5 * (1.0 + lax.erf(pre * ROOT_HALF)) + pre * jnp.exp(-0.5 * pre * pre) * INV_ROOT_TAU

def angle_tables(positions):
    half = ROT // 2
    freq = jnp.power(10000.0, -jnp.arange(half, dtype=jnp.float32) * (2.0 / ROT))
    angle = positions.astype(jnp.float32)[..., None] * freq
    cosine = jnp.cos(angle)
    sine = jnp.sin(angle)
    return (jnp.concatenate([cosine, cosine], -1)[:, :, None, :], jnp.concatenate([sine, sine], -1)[:, :, None, :])

def turn(vec, cosine, sine):
    half = ROT // 2
    head = vec[..., :ROT]
    swapped = jnp.concatenate([-head[..., half:], head[..., :half]], -1)
    return jnp.concatenate([head * cosine + swapped * sine, vec[..., ROT:]], -1)

def turn_back(grad, cosine, sine):
    half = ROT // 2
    head = grad[..., :ROT]
    scaled = head * sine
    back = jnp.concatenate([scaled[..., half:], -scaled[..., :half]], -1)
    return jnp.concatenate([head * cosine + back, grad[..., ROT:]], -1)

def attention_mask(segs):
    index = jnp.arange(segs.shape[-1])
    causal = index[None, :, None] >= index[None, None, :]
    return (segs[:, :, None] == segs[:, None, :]) & causal

def reference(layer_input, out_grad, segments, positions, qkv_weight, qkv_bias, dense_weight, dense_bias, inner_weight, inner_bias, outer_weight, outer_bias, attention_norm_gain, attention_norm_bias, feedforward_norm_gain, feedforward_norm_bias):
    blocks = MB * N_FSDP
    block_rows = SEQ_MB * LEN
    scale = HD ** (-0.5)
    qkv_b = qkv_bias.reshape(-1).astype(jnp.float32)
    inner_b = inner_bias.reshape(-1).astype(jnp.float32)

    def step(carry, block):
        layer_token_rows, grad_rows, segs, poss = block
        seqs = segs.shape[0]
        normalized_input, inverse_deviation = normalize_rows(layer_token_rows)
        first_branch = (normalized_input * attention_norm_gain + attention_norm_bias).astype(jnp.bfloat16)
        second_branch = (normalized_input * feedforward_norm_gain + feedforward_norm_bias).astype(jnp.bfloat16)
        packed = jnp.dot(first_branch, qkv_weight, preferred_element_type=jnp.float32) + qkv_b
        packed = packed.reshape(seqs, LEN, H, 3, HD)
        cosine, sine = angle_tables(poss)
        query = turn(packed[:, :, :, 0], cosine, sine).astype(jnp.bfloat16)
        keyed = turn(packed[:, :, :, 1], cosine, sine).astype(jnp.bfloat16)
        value = packed[:, :, :, 2].astype(jnp.bfloat16)
        query_f = query.astype(jnp.float32)
        keyed_f = keyed.astype(jnp.float32)
        value_f = value.astype(jnp.float32)
        mask = attention_mask(segs)[:, None]
        scores = jnp.where(mask, jnp.einsum('sqhd,skhd->shqk', query_f, keyed_f) * scale, MASKED)
        peak = lax.optimization_barrier(jnp.max(scores, -1, keepdims=True))
        log_total = peak + jnp.log(lax.optimization_barrier(jnp.sum(jnp.exp(scores - peak), -1, keepdims=True)))
        probs = jnp.exp(scores - log_total)
        probs_b = lax.optimization_barrier(probs.astype(jnp.bfloat16)).astype(jnp.float32)
        context = jnp.einsum('shqk,skhd->sqhd', probs_b, value_f).astype(jnp.bfloat16)
        flat_ctx = context.reshape(seqs * LEN, D)
        attn = jnp.dot(flat_ctx, dense_weight, preferred_element_type=jnp.float32)
        pre = jnp.dot(second_branch, inner_weight, preferred_element_type=jnp.float32) + inner_b
        act = gelu_value(pre).astype(jnp.bfloat16)
        mlp = jnp.dot(act, outer_weight, preferred_element_type=jnp.float32)
        result = (layer_token_rows.astype(jnp.float32) + attn + mlp + dense_bias + outer_bias).astype(jnp.bfloat16)
        upstream_gradient = grad_rows.astype(jnp.float32)
        g_bias = lax.optimization_barrier(jnp.sum(upstream_gradient, 0))
        d_act = jnp.dot(grad_rows, outer_weight.T, preferred_element_type=jnp.float32)
        g_outer = jnp.dot(act.T, grad_rows, preferred_element_type=jnp.float32)
        d_pre = d_act * gelu_slope(pre)
        g_inner_b = lax.optimization_barrier(jnp.sum(d_pre, 0)).reshape(H, FF // H)
        d_pre_b = d_pre.astype(jnp.bfloat16)
        g_inner = jnp.dot(second_branch.T, d_pre_b, preferred_element_type=jnp.float32)
        second_branch_gradient = jnp.dot(d_pre_b, inner_weight.T, preferred_element_type=jnp.float32)
        d_ctx = jnp.dot(grad_rows, dense_weight.T, preferred_element_type=jnp.float32).astype(jnp.bfloat16)
        g_dense = jnp.dot(flat_ctx.T, grad_rows, preferred_element_type=jnp.float32)
        d_ctx_f = d_ctx.reshape(seqs, LEN, H, HD).astype(jnp.float32)
        delta = lax.optimization_barrier(jnp.sum(d_ctx_f * context.astype(jnp.float32), -1))
        d_probs = jnp.einsum('sqhd,skhd->shqk', d_ctx_f, value_f)
        d_scores = probs * (d_probs - jnp.transpose(delta, (0, 2, 1))[..., None])
        d_value = jnp.einsum('shqk,sqhd->skhd', probs_b, d_ctx_f)
        d_scores_b = lax.optimization_barrier(d_scores.astype(jnp.bfloat16)).astype(jnp.float32)
        d_query = jnp.einsum('shqk,skhd->sqhd', d_scores_b, keyed_f) * scale
        d_key = jnp.einsum('shqk,sqhd->skhd', d_scores_b, query_f) * scale
        d_packed = jnp.stack([turn_back(d_query, cosine, sine), turn_back(d_key, cosine, sine), d_value], 3)
        d_packed = d_packed.reshape(seqs * LEN, 3 * D)
        g_qkv_b = lax.optimization_barrier(jnp.sum(d_packed, 0)).reshape(H, 3 * HD)
        d_packed_b = d_packed.astype(jnp.bfloat16)
        g_qkv = jnp.dot(first_branch.T, d_packed_b, preferred_element_type=jnp.float32)
        first_branch_gradient = jnp.dot(d_packed_b, qkv_weight.T, preferred_element_type=jnp.float32)
        attention_gain_gradient = lax.optimization_barrier(jnp.sum(first_branch_gradient * normalized_input, 0))
        g_shift1 = lax.optimization_barrier(jnp.sum(first_branch_gradient, 0))
        feedforward_gain_gradient = lax.optimization_barrier(jnp.sum(second_branch_gradient * normalized_input, 0))
        g_shift2 = lax.optimization_barrier(jnp.sum(second_branch_gradient, 0))
        normalized_gradient = first_branch_gradient * attention_norm_gain + second_branch_gradient * feedforward_norm_gain
        input_gradient = upstream_gradient + inverse_deviation * (normalized_gradient - lax.optimization_barrier(jnp.mean(normalized_gradient, -1, keepdims=True)) - normalized_input * lax.optimization_barrier(jnp.mean(normalized_gradient * normalized_input, -1, keepdims=True)))
        adds = (g_qkv, g_qkv_b, g_dense, g_bias, g_inner, g_inner_b, g_outer, attention_gain_gradient, g_shift1, feedforward_gain_gradient, g_shift2)
        carry = tuple((c + a for c, a in zip(carry, adds)))
        return (carry, (result, input_gradient.astype(jnp.bfloat16)))
    init = (jnp.zeros((D, 3 * D), jnp.float32), jnp.zeros((H, 3 * HD), jnp.float32), jnp.zeros((D, D), jnp.float32), jnp.zeros((D,), jnp.float32), jnp.zeros((D, FF), jnp.float32), jnp.zeros((H, FF // H), jnp.float32), jnp.zeros((FF, D), jnp.float32), jnp.zeros((D,), jnp.float32), jnp.zeros((D,), jnp.float32), jnp.zeros((D,), jnp.float32), jnp.zeros((D,), jnp.float32))
    inputs = (layer_input.reshape(blocks, block_rows, D), out_grad.reshape(blocks, block_rows, D), segments.reshape(blocks, SEQ_MB, LEN), positions.reshape(blocks, SEQ_MB, LEN))
    sums, (results, grads_in) = lax.scan(step, init, inputs)
    g_qkv, g_qkv_b, g_dense, g_bias, g_inner, g_inner_b, g_outer, attention_gain_gradient, g_shift1, feedforward_gain_gradient, g_shift2 = sums
    return (results.reshape(MB, TOK_STEP, D), grads_in.reshape(MB, TOK_STEP, D), g_qkv, g_qkv_b, g_dense, g_bias, g_inner, g_inner_b, g_outer, g_bias, attention_gain_gradient, g_shift1, feedforward_gain_gradient, g_shift2)
```

```python
import jax
import jax.numpy as jnp
from jax import lax
from jax.sharding import PartitionSpec as P

H = 16
HD = 64
ROT = 16
FF = 4096


EPS = 1e-05
ROOT_HALF = 0.7071067811865476
INV_ROOT_TAU = 0.3989422804014327
MASKED = -1e30


def normalize_rows(token_row_block):
    values = token_row_block.astype(jnp.float32)
    centre = values - jnp.mean(values, -1, keepdims=True)
    scale = lax.rsqrt(jnp.mean(centre * centre, -1, keepdims=True) + EPS)
    return (centre * scale, scale)


def gelu_value(pre):
    return 0.5 * pre * (1.0 + lax.erf(pre * ROOT_HALF))


def gelu_slope(pre):
    return 0.5 * (1.0 + lax.erf(pre * ROOT_HALF)) + pre * jnp.exp(-0.5 * pre * pre) * INV_ROOT_TAU


def angle_tables(positions):
    half = ROT // 2
    freq = jnp.power(10000.0, -jnp.arange(half, dtype=jnp.float32) * (2.0 / ROT))
    angle = positions.astype(jnp.float32)[..., None] * freq
    cosine = jnp.cos(angle)
    sine = jnp.sin(angle)
    return (
        jnp.concatenate([cosine, cosine], -1)[:, :, None, :],
        jnp.concatenate([sine, sine], -1)[:, :, None, :],
    )


def turn(vec, cosine, sine):
    half = ROT // 2
    head = vec[..., :ROT]
    swapped = jnp.concatenate([-head[..., half:], head[..., :half]], -1)
    return jnp.concatenate([head * cosine + swapped * sine, vec[..., ROT:]], -1)


def turn_back(grad, cosine, sine):
    half = ROT // 2
    head = grad[..., :ROT]
    scaled = head * sine
    back = jnp.concatenate([scaled[..., half:], -scaled[..., :half]], -1)
    return jnp.concatenate([head * cosine + back, grad[..., ROT:]], -1)


def attention_mask(segs):
    index = jnp.arange(segs.shape[-1])
    causal = index[None, :, None] >= index[None, None, :]
    return (segs[:, :, None] == segs[:, None, :]) & causal


def matmul(left, right, left_dim, right_dim):
    return lax.dot_general(
        left, right, (((left_dim,), (right_dim,)), ((), ())), preferred_element_type=jnp.float32
    )


def unpack(gathered):
    qkv_w, qkv_b, dense_w, inner_w, inner_b, outer_w = gathered
    return (
        qkv_w,
        qkv_b.reshape(-1).astype(jnp.float32),
        dense_w,
        inner_w,
        inner_b.reshape(-1).astype(jnp.float32),
        outer_w,
    )


def raw_scores(query, keyed, mask, scale):
    product = jnp.einsum("sqhd,skhd->shqk", query, keyed, preferred_element_type=jnp.float32)
    return jnp.where(mask, product * scale, MASKED)


def plain_shards(
    layer_input,
    out_grad,
    segments,
    positions,
    qkv_weight,
    qkv_bias,
    dense_weight,
    dense_bias,
    inner_weight,
    inner_bias,
    outer_weight,
    outer_bias,
    attention_norm_gain,
    attention_norm_bias,
    feedforward_norm_gain,
    feedforward_norm_bias,
):
    attention_gain, attention_bias, feedforward_gain, feedforward_bias, bias_dense, bias_outer = (
        lax.all_gather(attention_norm_gain, ("fsdp", "tensor"), axis=0, tiled=True),
        lax.all_gather(attention_norm_bias, ("fsdp", "tensor"), axis=0, tiled=True),
        lax.all_gather(feedforward_norm_gain, ("fsdp", "tensor"), axis=0, tiled=True),
        lax.all_gather(feedforward_norm_bias, ("fsdp", "tensor"), axis=0, tiled=True),
        lax.all_gather(dense_bias, ("fsdp", "tensor"), axis=0, tiled=True),
        lax.all_gather(outer_bias, ("fsdp", "tensor"), axis=0, tiled=True),
    )
    scale = HD ** (-0.5)
    microbatch = 0
    weights = unpack(
        (
            lax.all_gather(qkv_weight, "fsdp", axis=0, tiled=True),
            lax.all_gather(qkv_bias, "fsdp", axis=1, tiled=True),
            lax.all_gather(dense_weight, "fsdp", axis=1, tiled=True),
            lax.all_gather(inner_weight, "fsdp", axis=0, tiled=True),
            lax.all_gather(inner_bias, "fsdp", axis=1, tiled=True),
            lax.all_gather(outer_weight, "fsdp", axis=1, tiled=True),
        )
    )
    qkv_w, qkv_b, dense_w, inner_w, inner_b, outer_w = weights
    token_row_block = lax.all_gather(layer_input[microbatch], "tensor", axis=0, tiled=True)
    segs = segments[microbatch]
    seqs, length = segs.shape
    heads = qkv_w.shape[1] // (3 * HD)
    normalized_input, unused_result = normalize_rows(token_row_block)
    first_branch = (normalized_input * attention_gain + attention_bias).astype(jnp.bfloat16)
    second_branch = (normalized_input * feedforward_gain + feedforward_bias).astype(jnp.bfloat16)
    packed = (jnp.dot(first_branch, qkv_w, preferred_element_type=jnp.float32) + qkv_b).reshape(
        seqs, length, heads, 3, HD
    )
    cosine, sine = angle_tables(positions[microbatch])
    query = turn(packed[:, :, :, 0], cosine, sine).astype(jnp.bfloat16)
    keyed = turn(packed[:, :, :, 1], cosine, sine).astype(jnp.bfloat16)
    value = packed[:, :, :, 2].astype(jnp.bfloat16)
    mask = attention_mask(segs)[:, None]
    scores = raw_scores(query, keyed, mask, scale)
    peak = jnp.max(scores, -1, keepdims=True)
    log_total = peak + jnp.log(jnp.sum(jnp.exp(scores - peak), -1, keepdims=True))
    probs_b = jnp.exp(scores - log_total).astype(jnp.bfloat16)
    context = jnp.einsum(
        "shqk,skhd->sqhd", probs_b, value, preferred_element_type=jnp.float32
    ).astype(jnp.bfloat16)
    flat_ctx = context.reshape(seqs * length, heads * HD)
    pre = jnp.dot(second_branch, inner_w, preferred_element_type=jnp.float32) + inner_b
    act = gelu_value(pre).astype(jnp.bfloat16)
    ctx_rows = flat_ctx
    act_rows = act
    mixed = lax.psum_scatter(
        (
            jnp.dot(ctx_rows, dense_w, preferred_element_type=jnp.float32)
            + jnp.dot(act_rows, outer_w, preferred_element_type=jnp.float32)
        ).astype(jnp.bfloat16),
        "tensor",
        scatter_dimension=0,
        tiled=True,
    ).astype(jnp.float32)
    outputs = [
        (layer_input[microbatch].astype(jnp.float32) + mixed + bias_dense + bias_outer).astype(
            jnp.bfloat16
        )
    ]
    saved = [
        (
            token_row_block,
            first_branch,
            second_branch,
            query,
            keyed,
            value,
            log_total,
            context,
            flat_ctx,
            pre,
            act,
        )
    ]
    g_qkv_b = jnp.zeros((qkv_bias.shape[0], 3 * HD), jnp.float32)
    g_inner_b = jnp.zeros((inner_bias.shape[0], FF // H), jnp.float32)
    microbatch = 0
    weights = unpack(
        (
            lax.all_gather(qkv_weight, "fsdp", axis=0, tiled=True),
            lax.all_gather(qkv_bias, "fsdp", axis=1, tiled=True),
            lax.all_gather(dense_weight, "fsdp", axis=1, tiled=True),
            lax.all_gather(inner_weight, "fsdp", axis=0, tiled=True),
            lax.all_gather(inner_bias, "fsdp", axis=1, tiled=True),
            lax.all_gather(outer_weight, "fsdp", axis=1, tiled=True),
        )
    )
    qkv_w, qkv_b, dense_w, inner_w, inner_b, outer_w = weights
    (
        token_row_block,
        first_branch,
        second_branch,
        query,
        keyed,
        value,
        log_total,
        context,
        flat_ctx,
        pre,
        act,
    ) = saved[microbatch]
    segs = segments[microbatch]
    seqs, length = segs.shape
    heads = qkv_w.shape[1] // (3 * HD)
    cot_rows = lax.all_gather(out_grad[microbatch], "tensor", axis=0, tiled=True)
    own_cot = out_grad[microbatch].astype(jnp.float32)
    g_bias = jnp.sum(own_cot, 0)
    d_act = matmul(cot_rows, outer_w, 1, 1)
    g_outer = matmul(act, cot_rows, 0, 0)
    d_pre = d_act * gelu_slope(pre)
    g_inner_b = jnp.sum(d_pre, 0).reshape(g_inner_b.shape)
    d_pre_b = d_pre.astype(jnp.bfloat16)
    g_inner = matmul(second_branch, d_pre_b, 0, 0)
    second_branch_gradient = matmul(d_pre_b, inner_w, 1, 1)
    d_ctx = matmul(cot_rows, dense_w, 1, 1).astype(jnp.bfloat16)
    g_dense = matmul(flat_ctx, cot_rows, 0, 0)
    d_ctx4 = d_ctx.reshape(context.shape)
    delta = jnp.sum(d_ctx4.astype(jnp.float32) * context.astype(jnp.float32), -1)
    mask = attention_mask(segs)[:, None]
    probs = jnp.exp(raw_scores(query, keyed, mask, scale) - log_total)
    d_probs = jnp.einsum("sqhd,skhd->shqk", d_ctx4, value, preferred_element_type=jnp.float32)
    d_scores = probs * (d_probs - jnp.transpose(delta, (0, 2, 1))[..., None])
    d_value = jnp.einsum(
        "shqk,sqhd->skhd", probs.astype(jnp.bfloat16), d_ctx4, preferred_element_type=jnp.float32
    )
    d_scores_b = d_scores.astype(jnp.bfloat16)
    d_query = (
        jnp.einsum("shqk,skhd->sqhd", d_scores_b, keyed, preferred_element_type=jnp.float32) * scale
    )
    d_key = (
        jnp.einsum("shqk,sqhd->skhd", d_scores_b, query, preferred_element_type=jnp.float32) * scale
    )
    cosine, sine = angle_tables(positions[microbatch])
    d_packed = jnp.stack(
        [turn_back(d_query, cosine, sine), turn_back(d_key, cosine, sine), d_value], 3
    )
    d_packed = d_packed.reshape(seqs * length, heads * 3 * HD)
    g_qkv_b = jnp.sum(d_packed, 0).reshape(g_qkv_b.shape)
    d_packed_b = d_packed.astype(jnp.bfloat16)
    g_qkv = matmul(first_branch, d_packed_b, 0, 0)
    first_branch_gradient = matmul(d_packed_b, qkv_w, 1, 1)
    local_normalized_input, local_inverse_deviation = normalize_rows(layer_input[microbatch])
    local_first_branch = lax.psum_scatter(
        first_branch_gradient.astype(jnp.bfloat16), "tensor", scatter_dimension=0, tiled=True
    ).astype(jnp.float32)
    local_second_branch = lax.psum_scatter(
        second_branch_gradient.astype(jnp.bfloat16), "tensor", scatter_dimension=0, tiled=True
    ).astype(jnp.float32)
    attention_gain_gradient = jnp.sum(local_first_branch * local_normalized_input, 0)
    g_shift1 = jnp.sum(local_first_branch, 0)
    feedforward_gain_gradient = jnp.sum(local_second_branch * local_normalized_input, 0)
    g_shift2 = jnp.sum(local_second_branch, 0)
    normalized_gradient = (
        local_first_branch * attention_gain + local_second_branch * feedforward_gain
    )
    input_gradient = own_cot + local_inverse_deviation * (
        normalized_gradient
        - jnp.mean(normalized_gradient, -1, keepdims=True)
        - local_normalized_input
        * jnp.mean(normalized_gradient * local_normalized_input, -1, keepdims=True)
    )
    in_grads = [input_gradient.astype(jnp.bfloat16)]
    s_qkv, s_qkv_b, s_dense, s_inner, s_inner_b, s_outer = (
        lax.psum_scatter(
            g_qkv.astype(jnp.bfloat16), "fsdp", scatter_dimension=0, tiled=True
        ).astype(jnp.float32),
        lax.psum_scatter(
            g_qkv_b.astype(jnp.bfloat16), "fsdp", scatter_dimension=1, tiled=True
        ).astype(jnp.float32),
        lax.psum_scatter(
            g_dense.astype(jnp.bfloat16), "fsdp", scatter_dimension=1, tiled=True
        ).astype(jnp.float32),
        lax.psum_scatter(
            g_inner.astype(jnp.bfloat16), "fsdp", scatter_dimension=0, tiled=True
        ).astype(jnp.float32),
        lax.psum_scatter(
            g_inner_b.astype(jnp.bfloat16), "fsdp", scatter_dimension=1, tiled=True
        ).astype(jnp.float32),
        lax.psum_scatter(
            g_outer.astype(jnp.bfloat16), "fsdp", scatter_dimension=1, tiled=True
        ).astype(jnp.float32),
    )
    s_bias, s_gain1, s_shift1, s_gain2, s_shift2 = (
        lax.psum_scatter(g_bias, ("fsdp", "tensor"), scatter_dimension=0, tiled=True),
        lax.psum_scatter(
            attention_gain_gradient, ("fsdp", "tensor"), scatter_dimension=0, tiled=True
        ),
        lax.psum_scatter(g_shift1, ("fsdp", "tensor"), scatter_dimension=0, tiled=True),
        lax.psum_scatter(
            feedforward_gain_gradient, ("fsdp", "tensor"), scatter_dimension=0, tiled=True
        ),
        lax.psum_scatter(g_shift2, ("fsdp", "tensor"), scatter_dimension=0, tiled=True),
    )
    return (
        jnp.stack(outputs),
        jnp.stack(in_grads),
        s_qkv,
        s_qkv_b,
        s_dense,
        s_bias,
        s_inner,
        s_inner_b,
        s_outer,
        s_bias,
        s_gain1,
        s_shift1,
        s_gain2,
        s_shift2,
    )


def core_swap(value):
    count = lax.axis_size("fsdp")
    return lax.ppermute(value, "fsdp", [(i, i ^ 1) for i in range(count)])


def near_swap(value):
    count = lax.axis_size("fsdp")
    return lax.ppermute(value, "fsdp", [(i, i ^ (4 if i & 1 else 2)) for i in range(count)])


def far_swap(value):
    count = lax.axis_size("fsdp")
    return lax.ppermute(value, "fsdp", [(i, i ^ (2 if i & 1 else 4)) for i in range(count)])


def depth_swap(value, mask):
    count = lax.axis_size("tensor")
    return lax.ppermute(value, "tensor", [(i, i ^ mask) for i in range(count)])


def slot_masks():
    core = lax.axis_index("fsdp") & 1
    near = jnp.where(core == 0, 2, 4)
    far = 6 - near
    return [0, 1, near, near + 1, far, far + 1, 6, 7]


def gather_blocks(shard):
    partner = core_swap(shard)
    near = near_swap(jnp.stack([shard, partner]))
    across = far_swap(near[0])
    far = core_swap(near)
    across_partner = core_swap(across)
    return [shard, partner, near[0], near[1], far[1], far[0], across, across_partner]


def in_order(slots):
    me = lax.axis_index("fsdp")
    core = me & 1
    stacked = jnp.stack(slots)
    ordered = []
    for k in range(len(slots)):
        mask = me ^ k
        middle = (mask >= 2) & (mask < 6)
        slot = jnp.where((core == 1) & middle, mask ^ 6, mask)
        ordered.append(lax.dynamic_index_in_dim(stacked, slot, 0, keepdims=False))
    return ordered


def scatter_sum(keep, send):
    kept = keep.astype(jnp.float32) + core_swap(send).astype(jnp.float32)
    across = far_swap(kept[3].astype(jnp.bfloat16))
    pair = jnp.stack([kept[1] + across.astype(jnp.float32), kept[2]]).astype(jnp.bfloat16)
    near = near_swap(pair)
    far = core_swap(near[1])
    return kept[0] + near[0].astype(jnp.float32) + far.astype(jnp.float32)


def split_blocks(blocks):
    me = lax.axis_index("fsdp")
    masks = slot_masks()
    pick = lambda s: lax.dynamic_index_in_dim(blocks, me ^ masks[s], 0, keepdims=False)
    return jnp.stack([pick(s) for s in (0, 2, 3, 6)]), jnp.stack([pick(s) for s in (1, 5, 4, 7)])


def in_three(value):
    high = lax.reduce_precision(value, 8, 7)
    rest = value - high
    middle = lax.reduce_precision(rest, 8, 7)
    return jnp.concatenate([high, middle, rest - middle]).astype(jnp.bfloat16)


def pair_shards(
    layer_input,
    out_grad,
    segments,
    positions,
    qkv_weight,
    qkv_bias,
    dense_weight,
    dense_bias,
    inner_weight,
    inner_bias,
    outer_weight,
    outer_bias,
    attention_norm_gain,
    attention_norm_bias,
    feedforward_norm_gain,
    feedforward_norm_bias,
):
    n = lax.axis_size("fsdp")
    m = lax.axis_size("tensor")
    f = lax.axis_index("fsdp")
    t = lax.axis_index("tensor")
    x = layer_input[0]
    g = out_grad[0]
    rows, width = x.shape
    strip = width // n
    heads = qkv_bias.shape[0]
    qkv_cols = qkv_weight.shape[1]
    units = inner_weight.shape[1]
    lanes = attention_norm_gain.shape[0]
    scale = HD ** (-0.5)

    vectors = in_three(
        jnp.stack(
            [
                attention_norm_gain,
                attention_norm_bias,
                feedforward_norm_gain,
                feedforward_norm_bias,
                dense_bias + outer_bias,
            ]
        )
    )
    spread = lax.dynamic_update_slice(jnp.zeros((15, strip), jnp.bfloat16), vectors, (0, lanes * t))
    for bit in range(m.bit_length() - 1):
        spread = spread + depth_swap(spread, 1 << bit)
    qkv_row = lax.dynamic_update_slice(
        jnp.zeros((heads, 3 * HD), jnp.bfloat16), qkv_bias, (0, qkv_bias.shape[1] * f)
    ).reshape(-1, strip)
    inner_row = lax.dynamic_update_slice(
        jnp.zeros((heads, units // heads), jnp.bfloat16), inner_bias, (0, inner_bias.shape[1] * f)
    ).reshape(-1, strip)
    qkv_rows, inner_rows = qkv_row.shape[0], inner_row.shape[0]
    used = 15 + qkv_rows + inner_rows
    small = jnp.concatenate(
        [spread, qkv_row, inner_row, jnp.zeros((strip - used, strip), jnp.bfloat16)]
    )

    x_slots = [x] + [depth_swap(x, k) for k in range(1, m)]
    outer_parts = [outer_weight[strip * i : strip * (i + 1)] for i in range(units // strip)]
    dense_parts = [dense_weight[strip * i : strip * (i + 1)] for i in range(heads * HD // strip)]
    second_msg = jnp.concatenate([inner_weight] + outer_parts + dense_parts, axis=1)
    first_msg = jnp.concatenate([qkv_weight, small], axis=1)
    second_blocks = in_order(gather_blocks(second_msg))
    first_blocks = in_order(gather_blocks(first_msg))
    g_slots = [g] + [depth_swap(g, k) for k in range(1, m)]

    qkv_w = jnp.concatenate([b[:, :qkv_cols] for b in first_blocks])
    smalls = jnp.stack([b[:, qkv_cols:] for b in first_blocks]).astype(jnp.float32)
    vec = smalls[:, 0:5] + smalls[:, 5:10] + smalls[:, 10:15]
    vec = jnp.transpose(vec, (1, 0, 2)).reshape(5, width)
    biases = jnp.sum(smalls[:, 15:used], 0)
    qkv_b = biases[:qkv_rows].reshape(-1)
    inner_b = biases[qkv_rows:].reshape(-1)
    inner_w = jnp.concatenate([b[:, :units] for b in second_blocks])

    def columns(start, count):
        return jnp.concatenate(
            [
                jnp.concatenate([b[:, start + strip * i : start + strip * (i + 1)] for b in second_blocks], axis=1)
                for i in range(count)
            ]
        )

    outer_w = columns(units, units // strip)
    dense_w = columns(2 * units, heads * HD // strip)

    pick = lambda a: jnp.concatenate([lax.dynamic_slice_in_dim(a, t ^ k, 1, 0) for k in range(m)])
    segs = pick(segments[0])
    poss = pick(positions[0])
    tokens = jnp.concatenate(x_slots)
    cot = jnp.concatenate(g_slots)
    xhat, rstd = normalize_rows(tokens)
    first = (xhat * vec[0] + vec[1]).astype(jnp.bfloat16)
    second = (xhat * vec[2] + vec[3]).astype(jnp.bfloat16)
    packed = (matmul(first, qkv_w, 1, 0) + qkv_b).reshape(m, rows, heads, 3, HD)
    cosine, sine = angle_tables(poss)
    query = turn(packed[:, :, :, 0], cosine, sine).astype(jnp.bfloat16)
    keyed = turn(packed[:, :, :, 1], cosine, sine).astype(jnp.bfloat16)
    value = packed[:, :, :, 2].astype(jnp.bfloat16)
    mask = attention_mask(segs)[:, None]
    scores = raw_scores(query, keyed, mask, scale)
    peak = jnp.max(scores, -1, keepdims=True)
    log_total = peak + jnp.log(jnp.sum(jnp.exp(scores - peak), -1, keepdims=True))
    probs = jnp.exp(scores - log_total)
    context = jnp.einsum(
        "shqk,skhd->sqhd", probs.astype(jnp.bfloat16), value, preferred_element_type=jnp.float32
    ).astype(jnp.bfloat16)
    flat_ctx = context.reshape(m * rows, heads * HD)
    pre = matmul(second, inner_w, 1, 0) + inner_b
    act = gelu_value(pre).astype(jnp.bfloat16)
    partial = matmul(flat_ctx, dense_w, 1, 0) + matmul(act, outer_w, 1, 0)
    result = x.astype(jnp.float32) + vec[4] + partial[:rows]
    for k in range(1, m):
        result = result + depth_swap(partial[rows * k : rows * (k + 1)].astype(jnp.bfloat16), k).astype(jnp.float32)

    d_act = matmul(cot, outer_w, 1, 1)
    g_outer = matmul(act, cot, 0, 0)
    d_pre = d_act * gelu_slope(pre)
    g_inner_b = jnp.sum(d_pre, 0)
    d_pre_b = d_pre.astype(jnp.bfloat16)
    g_inner = matmul(second, d_pre_b, 0, 0)
    d_second = matmul(d_pre_b, inner_w, 1, 1)
    big = jnp.stack(
        [
            jnp.concatenate(
                [g_inner[strip * k : strip * (k + 1)]]
                + [g_outer[strip * i : strip * (i + 1), strip * k : strip * (k + 1)] for i in range(units // strip)],
                axis=1,
            )
            for k in range(n)
        ]
    ).astype(jnp.bfloat16)
    big_sum = scatter_sum(*split_blocks(big))

    d_ctx = matmul(cot, dense_w, 1, 1).astype(jnp.bfloat16)
    g_dense = matmul(flat_ctx, cot, 0, 0)
    d_ctx4 = d_ctx.reshape(context.shape)
    delta = jnp.sum(d_ctx4.astype(jnp.float32) * context.astype(jnp.float32), -1)
    d_probs = jnp.einsum("sqhd,skhd->shqk", d_ctx4, value, preferred_element_type=jnp.float32)
    d_scores = probs * (d_probs - jnp.transpose(delta, (0, 2, 1))[..., None])
    d_value = jnp.einsum(
        "shqk,sqhd->skhd", probs.astype(jnp.bfloat16), d_ctx4, preferred_element_type=jnp.float32
    )
    d_scores_b = d_scores.astype(jnp.bfloat16)
    d_query = (
        jnp.einsum("shqk,skhd->sqhd", d_scores_b, keyed, preferred_element_type=jnp.float32) * scale
    )
    d_key = (
        jnp.einsum("shqk,sqhd->skhd", d_scores_b, query, preferred_element_type=jnp.float32) * scale
    )
    d_packed = jnp.stack(
        [turn_back(d_query, cosine, sine), turn_back(d_key, cosine, sine), d_value], 3
    ).reshape(m * rows, qkv_cols)
    g_qkv_b = jnp.sum(d_packed, 0)
    d_packed_b = d_packed.astype(jnp.bfloat16)
    g_qkv = matmul(first, d_packed_b, 0, 0)
    d_first = matmul(d_packed_b, qkv_w, 1, 1)

    own = g.astype(jnp.float32)
    sums = jnp.stack(
        [
            jnp.sum(own, 0),
            jnp.sum(d_first * xhat, 0),
            jnp.sum(d_first, 0),
            jnp.sum(d_second * xhat, 0),
            jnp.sum(d_second, 0),
        ]
    )
    for bit in range(m.bit_length() - 1):
        sums = sums + depth_swap(sums, 1 << bit)
    d_norm = d_first * vec[0] + d_second * vec[2]
    local_norm = d_norm[:rows]
    for k in range(1, m):
        local_norm = local_norm + depth_swap(d_norm[rows * k : rows * (k + 1)].astype(jnp.bfloat16), k).astype(jnp.float32)
    local_xhat, local_rstd = xhat[:rows], rstd[:rows]
    input_gradient = own + local_rstd * (
        local_norm
        - jnp.mean(local_norm, -1, keepdims=True)
        - local_xhat * jnp.mean(local_norm * local_xhat, -1, keepdims=True)
    )
    rest = jnp.stack(
        [
            jnp.concatenate(
                [g_qkv[strip * k : strip * (k + 1)]]
                + [g_dense[strip * i : strip * (i + 1), strip * k : strip * (k + 1)] for i in range(heads * HD // strip)]
                + [
                    jnp.concatenate(
                        [
                            sums[:, strip * k : strip * (k + 1)],
                            g_qkv_b.reshape(-1, strip),
                            g_inner_b.reshape(-1, strip),
                            jnp.zeros((strip - 5 - qkv_rows - inner_rows, strip), jnp.float32),
                        ]
                    )
                ],
                axis=1,
            )
            for k in range(n)
        ]
    ).astype(jnp.bfloat16)
    rest_sum = scatter_sum(*split_blocks(rest))
    s_inner = big_sum[:, :units]
    s_outer = jnp.concatenate([big_sum[:, units + strip * i : units + strip * (i + 1)] for i in range(units // strip)])
    s_qkv = rest_sum[:, :qkv_cols]
    at = qkv_cols
    s_dense = jnp.concatenate([rest_sum[:, at + strip * i : at + strip * (i + 1)] for i in range(heads * HD // strip)])
    tiny = rest_sum[:, qkv_cols + heads * HD :]
    five = lax.dynamic_slice(tiny, (0, lanes * t), (5, lanes))
    s_qkv_b = lax.dynamic_slice_in_dim(
        tiny[5 : 5 + qkv_rows].reshape(heads, 3 * HD), qkv_bias.shape[1] * f, qkv_bias.shape[1], 1
    )
    s_inner_b = lax.dynamic_slice_in_dim(
        tiny[5 + qkv_rows : 5 + qkv_rows + inner_rows].reshape(heads, units // heads),
        inner_bias.shape[1] * f,
        inner_bias.shape[1],
        1,
    )
    return (
        result.astype(jnp.bfloat16)[None],
        input_gradient.astype(jnp.bfloat16)[None],
        s_qkv,
        s_qkv_b,
        s_dense,
        five[0],
        s_inner,
        s_inner_b,
        s_outer,
        five[0],
        five[1],
        five[2],
        five[3],
        five[4],
    )


def solution(mesh):
    n, m = mesh.shape["fsdp"], mesh.shape["tensor"]
    shards = pair_shards if n == 8 and m & (m - 1) == 0 else plain_shards
    placed = (
        P(None, ("fsdp", "tensor"), None),
        P(None, ("fsdp", "tensor"), None),
        P(None, "fsdp", None),
        P(None, "fsdp", None),
        P("fsdp", "tensor"),
        P("tensor", "fsdp"),
        P("tensor", "fsdp"),
        P(("fsdp", "tensor")),
        P("fsdp", "tensor"),
        P("tensor", "fsdp"),
        P("tensor", "fsdp"),
        P(("fsdp", "tensor")),
        P(("fsdp", "tensor")),
        P(("fsdp", "tensor")),
        P(("fsdp", "tensor")),
        P(("fsdp", "tensor")),
    )
    return jax.shard_map(
        shards,
        mesh=mesh,
        in_specs=placed,
        out_specs=(
            P(None, ("fsdp", "tensor"), None),
            P(None, ("fsdp", "tensor"), None),
            P("fsdp", "tensor"),
            P("tensor", "fsdp"),
            P("tensor", "fsdp"),
            P(("fsdp", "tensor")),
            P("fsdp", "tensor"),
            P("tensor", "fsdp"),
            P("tensor", "fsdp"),
            P(("fsdp", "tensor")),
            P(("fsdp", "tensor")),
            P(("fsdp", "tensor")),
            P(("fsdp", "tensor")),
            P(("fsdp", "tensor")),
        ),
        check_vma=False,
    )
```

```python
import functools

import jax
import jax.numpy as jnp
from jax import lax
from jax.experimental import pallas as pl
from jax.experimental.pallas import tpu as pltpu
from jax.sharding import PartitionSpec as P

H = 16
HD = 64
ROT = 16
FF = 4096


EPS = 1e-05
ROOT_HALF = 0.7071067811865476
INV_ROOT_TAU = 0.3989422804014327
MASKED = -1e30
UNROLL = True
FSDP = "fsdp"
TENSOR = "tensor"
VMEM_LIMIT = 18 * 1024 * 1024


def normalize_rows(token_row_block):
    values = token_row_block.astype(jnp.float32)
    centre = values - jnp.mean(values, -1, keepdims=True)
    scale = lax.rsqrt(jnp.mean(centre * centre, -1, keepdims=True) + EPS)
    return (centre * scale, scale)


def gelu_value(pre):
    return 0.5 * pre * (1.0 + lax.erf(pre * ROOT_HALF))


def gelu_slope(pre):
    return 0.5 * (1.0 + lax.erf(pre * ROOT_HALF)) + pre * jnp.exp(-0.5 * pre * pre) * INV_ROOT_TAU


def angle_tables(positions):
    half = ROT // 2
    freq = jnp.power(10000.0, -jnp.arange(half, dtype=jnp.float32) * (2.0 / ROT))
    angle = positions.astype(jnp.float32)[..., None] * freq
    cosine = jnp.cos(angle)
    sine = jnp.sin(angle)
    return (
        jnp.concatenate([cosine, cosine], -1)[:, :, None, :],
        jnp.concatenate([sine, sine], -1)[:, :, None, :],
    )


def turn(vec, cosine, sine):
    half = ROT // 2
    head = vec[..., :ROT]
    swapped = jnp.concatenate([-head[..., half:], head[..., :half]], -1)
    return jnp.concatenate([head * cosine + swapped * sine, vec[..., ROT:]], -1)


def turn_back(grad, cosine, sine):
    half = ROT // 2
    head = grad[..., :ROT]
    scaled = head * sine
    back = jnp.concatenate([scaled[..., half:], -scaled[..., :half]], -1)
    return jnp.concatenate([head * cosine + back, grad[..., ROT:]], -1)


def attention_mask(segs):
    index = jnp.arange(segs.shape[-1])
    causal = index[None, :, None] >= index[None, None, :]
    return (segs[:, :, None] == segs[:, None, :]) & causal


def matmul(left, right, left_dim, right_dim):
    return lax.dot_general(
        left, right, (((left_dim,), (right_dim,)), ((), ())), preferred_element_type=jnp.float32
    )


def unpack(gathered):
    qkv_w, qkv_b, dense_w, inner_w, inner_b, outer_w = gathered
    return (
        qkv_w,
        qkv_b.reshape(-1).astype(jnp.float32),
        dense_w,
        inner_w,
        inner_b.reshape(-1).astype(jnp.float32),
        outer_w,
    )


def raw_scores(query, keyed, mask, scale):
    product = jnp.einsum("sqhd,skhd->shqk", query, keyed, preferred_element_type=jnp.float32)
    return jnp.where(mask, product * scale, MASKED)


def plain_shards(
    layer_input,
    out_grad,
    segments,
    positions,
    qkv_weight,
    qkv_bias,
    dense_weight,
    dense_bias,
    inner_weight,
    inner_bias,
    outer_weight,
    outer_bias,
    attention_norm_gain,
    attention_norm_bias,
    feedforward_norm_gain,
    feedforward_norm_bias,
):
    attention_gain, attention_bias, feedforward_gain, feedforward_bias, bias_dense, bias_outer = (
        lax.all_gather(attention_norm_gain, (FSDP, TENSOR), axis=0, tiled=True),
        lax.all_gather(attention_norm_bias, (FSDP, TENSOR), axis=0, tiled=True),
        lax.all_gather(feedforward_norm_gain, (FSDP, TENSOR), axis=0, tiled=True),
        lax.all_gather(feedforward_norm_bias, (FSDP, TENSOR), axis=0, tiled=True),
        lax.all_gather(dense_bias, (FSDP, TENSOR), axis=0, tiled=True),
        lax.all_gather(outer_bias, (FSDP, TENSOR), axis=0, tiled=True),
    )
    scale = HD ** (-0.5)
    microbatch = 0
    weights = unpack(
        (
            lax.all_gather(qkv_weight, FSDP, axis=0, tiled=True),
            lax.all_gather(qkv_bias, FSDP, axis=1, tiled=True),
            lax.all_gather(dense_weight, FSDP, axis=1, tiled=True),
            lax.all_gather(inner_weight, FSDP, axis=0, tiled=True),
            lax.all_gather(inner_bias, FSDP, axis=1, tiled=True),
            lax.all_gather(outer_weight, FSDP, axis=1, tiled=True),
        )
    )
    qkv_w, qkv_b, dense_w, inner_w, inner_b, outer_w = weights
    token_row_block = lax.all_gather(layer_input[microbatch], TENSOR, axis=0, tiled=True)
    segs = segments[microbatch]
    seqs, length = segs.shape
    heads = qkv_w.shape[1] // (3 * HD)
    normalized_input, _ = normalize_rows(token_row_block)
    first_branch = (normalized_input * attention_gain + attention_bias).astype(jnp.bfloat16)
    second_branch = (normalized_input * feedforward_gain + feedforward_bias).astype(jnp.bfloat16)
    packed = (jnp.dot(first_branch, qkv_w, preferred_element_type=jnp.float32) + qkv_b).reshape(
        seqs, length, heads, 3, HD
    )
    cosine, sine = angle_tables(positions[microbatch])
    query = turn(packed[:, :, :, 0], cosine, sine).astype(jnp.bfloat16)
    keyed = turn(packed[:, :, :, 1], cosine, sine).astype(jnp.bfloat16)
    value = packed[:, :, :, 2].astype(jnp.bfloat16)
    mask = attention_mask(segs)[:, None]
    scores = raw_scores(query, keyed, mask, scale)
    peak = jnp.max(scores, -1, keepdims=True)
    log_total = peak + jnp.log(jnp.sum(jnp.exp(scores - peak), -1, keepdims=True))
    probs_b = jnp.exp(scores - log_total).astype(jnp.bfloat16)
    context = jnp.einsum(
        "shqk,skhd->sqhd", probs_b, value, preferred_element_type=jnp.float32
    ).astype(jnp.bfloat16)
    flat_ctx = context.reshape(seqs * length, heads * HD)
    pre = jnp.dot(second_branch, inner_w, preferred_element_type=jnp.float32) + inner_b
    act = gelu_value(pre).astype(jnp.bfloat16)
    ctx_rows = flat_ctx
    act_rows = act
    mixed = lax.psum_scatter(
        (
            jnp.dot(ctx_rows, dense_w, preferred_element_type=jnp.float32)
            + jnp.dot(act_rows, outer_w, preferred_element_type=jnp.float32)
        ).astype(jnp.bfloat16),
        TENSOR,
        scatter_dimension=0,
        tiled=True,
    ).astype(jnp.float32)
    outputs = [
        (layer_input[microbatch].astype(jnp.float32) + mixed + bias_dense + bias_outer).astype(
            jnp.bfloat16
        )
    ]
    saved = [
        (
            token_row_block,
            first_branch,
            second_branch,
            query,
            keyed,
            value,
            log_total,
            context,
            flat_ctx,
            pre,
            act,
        )
    ]
    g_qkv_b = jnp.zeros((qkv_bias.shape[0], 3 * HD), jnp.float32)
    g_inner_b = jnp.zeros((inner_bias.shape[0], FF // H), jnp.float32)
    microbatch = 0
    weights = unpack(
        (
            lax.all_gather(qkv_weight, FSDP, axis=0, tiled=True),
            lax.all_gather(qkv_bias, FSDP, axis=1, tiled=True),
            lax.all_gather(dense_weight, FSDP, axis=1, tiled=True),
            lax.all_gather(inner_weight, FSDP, axis=0, tiled=True),
            lax.all_gather(inner_bias, FSDP, axis=1, tiled=True),
            lax.all_gather(outer_weight, FSDP, axis=1, tiled=True),
        )
    )
    qkv_w, qkv_b, dense_w, inner_w, inner_b, outer_w = weights
    (
        token_row_block,
        first_branch,
        second_branch,
        query,
        keyed,
        value,
        log_total,
        context,
        flat_ctx,
        pre,
        act,
    ) = saved[microbatch]
    segs = segments[microbatch]
    seqs, length = segs.shape
    heads = qkv_w.shape[1] // (3 * HD)
    cot_rows = lax.all_gather(out_grad[microbatch], TENSOR, axis=0, tiled=True)
    own_cot = out_grad[microbatch].astype(jnp.float32)
    g_bias = jnp.sum(own_cot, 0)
    d_act = matmul(cot_rows, outer_w, 1, 1)
    g_outer = matmul(act, cot_rows, 0, 0)
    d_pre = d_act * gelu_slope(pre)
    g_inner_b = jnp.sum(d_pre, 0).reshape(g_inner_b.shape)
    d_pre_b = d_pre.astype(jnp.bfloat16)
    g_inner = matmul(second_branch, d_pre_b, 0, 0)
    second_branch_gradient = matmul(d_pre_b, inner_w, 1, 1)
    d_ctx = matmul(cot_rows, dense_w, 1, 1).astype(jnp.bfloat16)
    g_dense = matmul(flat_ctx, cot_rows, 0, 0)
    d_ctx4 = d_ctx.reshape(context.shape)
    delta = jnp.sum(d_ctx4.astype(jnp.float32) * context.astype(jnp.float32), -1)
    mask = attention_mask(segs)[:, None]
    probs = jnp.exp(raw_scores(query, keyed, mask, scale) - log_total)
    d_probs = jnp.einsum("sqhd,skhd->shqk", d_ctx4, value, preferred_element_type=jnp.float32)
    d_scores = probs * (d_probs - jnp.transpose(delta, (0, 2, 1))[..., None])
    d_value = jnp.einsum(
        "shqk,sqhd->skhd", probs.astype(jnp.bfloat16), d_ctx4, preferred_element_type=jnp.float32
    )
    d_scores_b = d_scores.astype(jnp.bfloat16)
    d_query = (
        jnp.einsum("shqk,skhd->sqhd", d_scores_b, keyed, preferred_element_type=jnp.float32) * scale
    )
    d_key = (
        jnp.einsum("shqk,sqhd->skhd", d_scores_b, query, preferred_element_type=jnp.float32) * scale
    )
    cosine, sine = angle_tables(positions[microbatch])
    d_packed = jnp.stack(
        [turn_back(d_query, cosine, sine), turn_back(d_key, cosine, sine), d_value], 3
    )
    d_packed = d_packed.reshape(seqs * length, heads * 3 * HD)
    g_qkv_b = jnp.sum(d_packed, 0).reshape(g_qkv_b.shape)
    d_packed_b = d_packed.astype(jnp.bfloat16)
    g_qkv = matmul(first_branch, d_packed_b, 0, 0)
    first_branch_gradient = matmul(d_packed_b, qkv_w, 1, 1)
    local_normalized_input, local_inverse_deviation = normalize_rows(layer_input[microbatch])
    local_first_branch = lax.psum_scatter(
        first_branch_gradient.astype(jnp.bfloat16), TENSOR, scatter_dimension=0, tiled=True
    ).astype(jnp.float32)
    local_second_branch = lax.psum_scatter(
        second_branch_gradient.astype(jnp.bfloat16), TENSOR, scatter_dimension=0, tiled=True
    ).astype(jnp.float32)
    attention_gain_gradient = jnp.sum(local_first_branch * local_normalized_input, 0)
    g_shift1 = jnp.sum(local_first_branch, 0)
    feedforward_gain_gradient = jnp.sum(local_second_branch * local_normalized_input, 0)
    g_shift2 = jnp.sum(local_second_branch, 0)
    normalized_gradient = (
        local_first_branch * attention_gain + local_second_branch * feedforward_gain
    )
    input_gradient = own_cot + local_inverse_deviation * (
        normalized_gradient
        - jnp.mean(normalized_gradient, -1, keepdims=True)
        - local_normalized_input
        * jnp.mean(normalized_gradient * local_normalized_input, -1, keepdims=True)
    )
    in_grads = [input_gradient.astype(jnp.bfloat16)]
    s_qkv, s_qkv_b, s_dense, s_inner, s_inner_b, s_outer = (
        lax.psum_scatter(
            g_qkv.astype(jnp.bfloat16), FSDP, scatter_dimension=0, tiled=True
        ).astype(jnp.float32),
        lax.psum_scatter(
            g_qkv_b.astype(jnp.bfloat16), FSDP, scatter_dimension=1, tiled=True
        ).astype(jnp.float32),
        lax.psum_scatter(
            g_dense.astype(jnp.bfloat16), FSDP, scatter_dimension=1, tiled=True
        ).astype(jnp.float32),
        lax.psum_scatter(
            g_inner.astype(jnp.bfloat16), FSDP, scatter_dimension=0, tiled=True
        ).astype(jnp.float32),
        lax.psum_scatter(
            g_inner_b.astype(jnp.bfloat16), FSDP, scatter_dimension=1, tiled=True
        ).astype(jnp.float32),
        lax.psum_scatter(
            g_outer.astype(jnp.bfloat16), FSDP, scatter_dimension=1, tiled=True
        ).astype(jnp.float32),
    )
    s_bias, s_gain1, s_shift1, s_gain2, s_shift2 = (
        lax.psum_scatter(g_bias, (FSDP, TENSOR), scatter_dimension=0, tiled=True),
        lax.psum_scatter(
            attention_gain_gradient, (FSDP, TENSOR), scatter_dimension=0, tiled=True
        ),
        lax.psum_scatter(g_shift1, (FSDP, TENSOR), scatter_dimension=0, tiled=True),
        lax.psum_scatter(
            feedforward_gain_gradient, (FSDP, TENSOR), scatter_dimension=0, tiled=True
        ),
        lax.psum_scatter(g_shift2, (FSDP, TENSOR), scatter_dimension=0, tiled=True),
    )
    return (
        jnp.stack(outputs),
        jnp.stack(in_grads),
        s_qkv,
        s_qkv_b,
        s_dense,
        s_bias,
        s_inner,
        s_inner_b,
        s_outer,
        s_bias,
        s_gain1,
        s_shift1,
        s_gain2,
        s_shift2,
    )


def swap(value, axis, partner):
    count = lax.axis_size(axis)
    return lax.ppermute(value, axis, [(i, partner(i)) for i in range(count)])


def core_swap(value):
    return swap(value, FSDP, lambda i: i ^ 1)


def near_swap(value):
    return swap(value, FSDP, lambda i: i ^ (4 if i & 1 else 2))


def far_swap(value):
    return swap(value, FSDP, lambda i: i ^ (2 if i & 1 else 4))


def depth_swap(value, mask):
    return swap(value, TENSOR, lambda i: i ^ mask)


def depth_gather(value):
    second = depth_swap(value, 2)
    first = depth_swap(value, 1)
    return [value, first, second, depth_swap(second, 1)]


def depth_scatter(parts):
    third = depth_swap(parts[3], 1)
    first = depth_swap(parts[1], 1)
    (second,) = call(
        one_sum_body, [(third.shape, jnp.bfloat16)], [jnp.zeros((1,), jnp.int32), parts[2], third]
    )
    return [parts[0], first, depth_swap(second, 2)]


def slot_masks():
    core = lax.axis_index(FSDP) & 1
    near = jnp.where(core == 0, 2, 4)
    far = 6 - near
    return [0, 1, near, near + 1, far, far + 1, 6, 7]


def gather_blocks(shard):
    partner = core_swap(shard)
    near_own = near_swap(shard)
    near_partner = near_swap(partner)
    across = far_swap(near_own)
    far_partner = core_swap(near_own)
    far_own = core_swap(near_partner)
    across_partner = core_swap(across)
    return [shard, partner, near_own, near_partner, far_own, far_partner, across, across_partner]


def scatter_sum(keep, send):
    shape = keep.shape[1:]
    got = core_swap(send)
    own, near_own, near_partner, across = call(
        four_sums_body, [(shape, jnp.bfloat16)] * 4, [jnp.zeros((1,), jnp.int32), keep, got]
    )
    across = far_swap(across)
    near_partner = near_swap(near_partner)
    (near_own,) = call(one_sum_body, [(shape, jnp.bfloat16)], [jnp.zeros((1,), jnp.int32), near_own, across])
    near_own = near_swap(near_own)
    far = core_swap(near_partner)
    return [own, near_own, far]


def turn_tables(positions):
    half = ROT // 2
    lane = jnp.arange(2 * HD) % HD
    freq = jnp.power(10000.0, -(lane % half).astype(jnp.float32) * (2.0 / ROT))
    angle = positions.astype(jnp.float32) * freq
    sine = jnp.sin(angle)
    return (
        jnp.where(lane < ROT, jnp.cos(angle), 1.0),
        jnp.where(lane < half, -sine, 0.0),
        jnp.where((lane >= half) & (lane < ROT), sine, 0.0),
    )


def erf_value(value):
    v = jnp.clip(value, -4.0, 4.0)
    s = v * v
    top = jnp.full_like(s, -2.72614225801306e-10)
    for c in (2.77068142495902e-08, -2.10102402082508e-06, -5.69250639462346e-05, -7.34990630326855e-04, -2.95459980854025e-03, -1.60960333262415e-02):
        top = top * s + c
    low = jnp.full_like(s, -1.45660718464996e-05)
    for c in (-2.13374055278905e-04, -1.68282697438203e-03, -7.37332916720468e-03, -1.42647390514189e-02):
        low = low * s + c
    return v * top / low


def call(body, outs, ins, scratch=(), final=False, loose=False):
    specs = [pl.BlockSpec(memory_space=pltpu.SMEM)] + [pl.BlockSpec(memory_space=pltpu.VMEM)] * (len(ins) - 1)
    return pl.pallas_call(
        body,
        out_shape=[jax.ShapeDtypeStruct(*out) if final else pltpu.VMEM(*out) for out in outs],
        in_specs=specs,
        out_specs=[pl.BlockSpec(memory_space=pltpu.VMEM)] * len(outs),
        scratch_shapes=list(scratch),
        compiler_params=pltpu.CompilerParams(vmem_limit_bytes=VMEM_LIMIT),
    )(ins[0], *[pltpu.with_memory_space_constraint(a, pltpu.HBM if loose else pltpu.VMEM) for a in ins[1:]])


def four_sums_body(scal, keep, got, *outs):
    for i, out in enumerate(outs):
        out[...] = (keep[i].astype(jnp.float32) + got[i].astype(jnp.float32)).astype(out.dtype)


def one_sum_body(scal, one, two, out):
    out[...] = (one[...].astype(jnp.float32) + two[...].astype(jnp.float32)).astype(out.dtype)


def pack_body(inner, outer, dense, x, g, message, x_copy, g_copy):
    x_copy[...] = x[...]
    g_copy[...] = g[...]
    strip, units = inner.shape
    message[:, :units] = inner[...]
    for i in range(outer.shape[0] // strip):
        message[:, units + strip * i : units + strip * (i + 1)] = outer[strip * i : strip * (i + 1), :]
    for i in range(dense.shape[0] // strip):
        message[:, 2 * units + strip * i : 2 * units + strip * (i + 1)] = dense[strip * i : strip * (i + 1), :]


def in_three(value):
    high = value.astype(jnp.bfloat16)
    rest = value - high.astype(jnp.float32)
    middle = rest.astype(jnp.bfloat16)
    return [part.astype(jnp.float32) for part in (high, middle, rest - middle.astype(jnp.float32))]


def placed(value, lanes, shift):
    rows, count = value.shape
    wide = jnp.concatenate([value, jnp.zeros((rows, lanes - count), value.dtype)], axis=1)
    return pltpu.roll(wide, shift, 1)


def pack_attend_body(scal, *refs):
    vectors, qkv, qkv_bias, inner_bias, message = refs[:6], refs[6], refs[7], refs[8], refs[9]
    strip, cols = qkv.shape
    lanes = vectors[0].shape[1]
    rows = [ref[...] for ref in vectors[:4]] + [vectors[4][...] + vectors[5][...]]
    parts = in_three(jnp.concatenate(rows, axis=0))
    three = jnp.concatenate(parts + [jnp.zeros((1, lanes), jnp.float32)], axis=0)
    biases = []
    for ref in (qkv_bias, inner_bias):
        value = placed(ref[...].astype(jnp.float32), 2 * strip, scal[9] * ref.shape[1])
        biases += [value[:, :strip], value[:, strip:]]
    small = jnp.concatenate([placed(three, strip, scal[8] * lanes)] + biases, axis=0)
    message[:, :cols] = qkv[...]
    message[:, cols:] = jnp.concatenate(
        [small, jnp.zeros((strip - small.shape[0], strip), jnp.float32)], axis=0
    ).astype(jnp.bfloat16)


def share_body(cols, scal, *refs):
    blocks, out = refs[:-1], refs[-1]
    for i, block in enumerate(blocks):
        out[i] = block[0:16, cols:]


def unpack_big_body(units, wide, scal, own, near, far, inner, outer, dense):
    total = own[...].astype(jnp.float32) + near[...].astype(jnp.float32) + far[...].astype(jnp.float32)
    strip = total.shape[0]
    inner[...] = total[:, :units]
    for i in range(units // strip):
        outer[strip * i : strip * (i + 1), :] = total[:, units + strip * i : units + strip * (i + 1)]
    for i in range(wide // strip):
        dense[strip * i : strip * (i + 1), :] = total[:, 2 * units + strip * i : 2 * units + strip * (i + 1)]


def unpack_rest_body(sizes, scal, own, near, far, qkv, qkv_b, inner_b, *fives):
    strip, cols, heads, lanes = sizes
    total = own[...].astype(jnp.float32) + near[...].astype(jnp.float32) + far[...].astype(jnp.float32)
    qkv[...] = total[:, :cols]
    tiny = total[:, cols:]
    for i, out in enumerate((qkv_b, inner_b)):
        at = 8 + 2 * heads * i
        pair = jnp.concatenate([tiny[at : at + heads], tiny[at + heads : at + 2 * heads]], axis=1)
        count = out.shape[1]
        out[...] = pltpu.roll(pair, 2 * strip - scal[9] * count, 1)[:, :count]
    for k, out in enumerate(fives):
        out[...] = pltpu.roll(tiny[0:8], strip - (scal[8] ^ k) * lanes, 1)[:, :lanes]


def result_body(m, scal, x, vec, *refs):
    total = x[...].astype(jnp.float32) + vec[4:5, :]
    for part in refs[:m]:
        total = total + part[...].astype(jnp.float32)
    refs[m][...] = total.astype(refs[m].dtype)


def standardize(values):
    centre = values - jnp.mean(values, -1, keepdims=True)
    scale = lax.rsqrt(jnp.mean(centre * centre, -1, keepdims=True) + EPS)
    return centre * scale, scale


def rotate(pair, cosine, low, high):
    lanes = pair.shape[-1]
    half = ROT // 2
    return pair * cosine + pltpu.roll(pair, lanes - half, 1) * low + pltpu.roll(pair, half, 1) * high


def rotate_back(pair, cosine, low, high):
    lanes = pair.shape[-1]
    half = ROT // 2
    return pair * cosine - pltpu.roll(pair, lanes - half, 1) * low - pltpu.roll(pair, half, 1) * high


def attend_body(m, heads, sizes, scal, *refs):
    strip, qkv_cols = sizes
    xs, blocks, shares = refs[:m], refs[m : m + 8], refs[m + 8 : 2 * m + 7]
    segs, cosine, low, high = refs[2 * m + 7 : 2 * m + 11]
    first, second, turned, probs, context, weight, vec, inner_b, smalls = refs[2 * m + 11 :]
    count = 8
    biases = jnp.zeros((4 * heads, strip), jnp.float32)
    for slot, view in enumerate(blocks):
        k = scal[slot]
        weight[pl.ds(pl.multiple_of(k * strip, strip), strip), :] = view[:, :qkv_cols]
        biases = biases + view[16 : 16 + 4 * heads, qkv_cols:].astype(jnp.float32)
        part = view[0:16, qkv_cols:].astype(jnp.float32)
        for share in shares:
            part = part + share[slot].astype(jnp.float32)
        smalls[k] = part
    for k in range(count):
        s = smalls[k]
        vec[0:5, strip * k : strip * (k + 1)] = s[0:5] + s[5:10] + s[10:15]
    rest = 3 * HD - strip
    qkv_b = jnp.concatenate(
        [piece for h in range(heads) for piece in (biases[h : h + 1], biases[heads + h : heads + h + 1, :rest])], axis=1
    )
    inner_b[...] = jnp.concatenate(
        [biases[at + h : at + h + 1] for h in range(heads) for at in (2 * heads, 3 * heads)], axis=1
    )
    rows = xs[0].shape[0]
    scale = HD ** (-0.5)
    after = lax.broadcasted_iota(jnp.int32, (rows, rows), 0) >= lax.broadcasted_iota(jnp.int32, (rows, rows), 1)
    for s in range(m):
        at = slice(rows * s, rows * (s + 1))
        xhat, _ = standardize(xs[s][...].astype(jnp.float32))
        one = (xhat * vec[0:1, :] + vec[1:2, :]).astype(jnp.bfloat16)
        first[at, :] = one
        second[at, :] = (xhat * vec[2:3, :] + vec[3:4, :]).astype(jnp.bfloat16)
    packed = jnp.dot(first[...], weight[...], preferred_element_type=jnp.float32) + qkv_b
    cos, lo, hi = cosine[...], low[...], high[...]
    for h in range(heads):
        base = 3 * HD * h
        pair = packed[:, base : base + 2 * HD]
        turned[:, base : base + 2 * HD] = rotate(pair, cos, lo, hi).astype(jnp.bfloat16)
        turned[:, base + 2 * HD : base + 3 * HD] = packed[:, base + 2 * HD : base + 3 * HD].astype(jnp.bfloat16)
    def one_sequence(s, unused):
        at = pl.ds(pl.multiple_of(s * rows, rows), rows)
        seg = jnp.broadcast_to(segs[pl.ds(scal[8] ^ s, 1), :].astype(jnp.float32), (rows, rows))
        mask = (seg == jnp.transpose(seg)) & after
        for h in range(heads):
            base = 3 * HD * h
            query = turned[at, base : base + HD]
            keyed = turned[at, base + HD : base + 2 * HD]
            value = turned[at, base + 2 * HD : base + 3 * HD]
            scores = jnp.where(mask, matmul(query, keyed, 1, 1) * scale, MASKED)
            peak = jnp.max(scores, -1, keepdims=True)
            raised = jnp.exp(scores - peak)
            prob = raised / jnp.sum(raised, -1, keepdims=True)
            probs[s * heads + h] = prob
            context[at, HD * h : HD * (h + 1)] = jnp.dot(
                prob.astype(jnp.bfloat16), value, preferred_element_type=jnp.float32
            ).astype(jnp.bfloat16)
        return unused

    lax.fori_loop(0, m, one_sequence, 0, unroll=UNROLL)


def feed_body(m, sizes, scal, *refs):
    strip, units, wide = sizes
    second, context, inner_b, blocks = refs[0], refs[1], refs[2], refs[3:11]
    inner, outer, dense, bend, act = refs[11:16]
    outs = refs[16:]
    for slot, view in enumerate(blocks):
        k = scal[slot]
        at = pl.ds(pl.multiple_of(k * strip, strip), strip)
        inner[at, :] = view[:, :units]
        for i in range(units // strip):
            outer[strip * i : strip * (i + 1), at] = view[:, units + strip * i : units + strip * (i + 1)]
        for i in range(wide // strip):
            dense[strip * i : strip * (i + 1), at] = view[:, 2 * units + strip * i : 2 * units + strip * (i + 1)]
    rows = outs[0].shape[0]
    for s in range(m):
        at = slice(rows * s, rows * (s + 1))
        value = jnp.dot(second[at, :], inner[...], preferred_element_type=jnp.float32) + inner_b[...]
        half = 0.5 * (1.0 + erf_value(value * ROOT_HALF))
        act[at, :] = (value * half).astype(jnp.bfloat16)
        bend[at, :] = half + value * jnp.exp(-0.5 * value * value) * INV_ROOT_TAU
    for s in range(m):
        at = slice(rows * s, rows * (s + 1))
        mixed = jnp.dot(act[at, :], outer[...], preferred_element_type=jnp.float32)
        mixed = mixed + jnp.dot(context[at, :], dense[...], preferred_element_type=jnp.float32)
        outs[s][...] = mixed.astype(outs[s].dtype)


def destinations(scal, keep, send):
    places = [(scal[slot], keep.at[j]) for j, slot in enumerate((0, 2, 3, 6))]
    places += [(scal[slot], send.at[j]) for j, slot in enumerate((1, 5, 4, 7))]
    return [places[i : i + 2] for i in range(0, len(places), 2)]


def two_blocks(source, pair, strip):
    return jnp.concatenate(
        [source[:, pl.ds(pl.multiple_of(k * strip, strip), strip)] for k, unused_result in pair], axis=1
    )


def feed_back_body(m, sizes, scal, *refs):
    strip, units, wide = sizes
    gs = refs[:m]
    act, bend, second, context, outer = refs[m : m + 5]
    keep, send, slope, g_inner_b, cot = refs[m + 5 :]
    rows = gs[0].shape[0]
    for s in range(m):
        cot[rows * s : rows * (s + 1), :] = gs[s][...]
    pairs = destinations(scal, keep, send)
    for pair in pairs:
        columns = two_blocks(cot, pair, strip)
        for source, count, start in ((act, units, units), (context, wide, 2 * units)):
            grad = matmul(source[...], columns, 0, 0).astype(jnp.bfloat16)
            for j, (unused_result, place) in enumerate(pair):
                for i in range(count // strip):
                    place[:, start + strip * i : start + strip * (i + 1)] = grad[
                        strip * i : strip * (i + 1), strip * j : strip * (j + 1)
                    ]
    total = jnp.zeros((1, units), jnp.float32)
    for s in range(m):
        at = slice(rows * s, rows * (s + 1))
        grad = matmul(cot[at, :], outer[...], 1, 1) * bend[at, :]
        total = total + jnp.sum(grad, 0, keepdims=True)
        slope[at, :] = grad.astype(jnp.bfloat16)
    g_inner_b[...] = total
    for pair in pairs:
        grad = matmul(two_blocks(second, pair, strip), slope[...], 0, 0).astype(jnp.bfloat16)
        for j, (unused_result, place) in enumerate(pair):
            place[:, :units] = grad[strip * j : strip * (j + 1)]


def attend_back_body(start, stop, heads, scal, *refs):
    cot, context, dense, turned, probs, cosine, low, high = refs[:8]
    d_packed_b, qkv_grad, d_packed, d_context = refs[8:]
    rows = d_context.shape[0] // (stop - start)
    scale = HD ** (-0.5)
    d_context[...] = matmul(cot[rows * start : rows * stop, :], dense[...], 1, 1).astype(jnp.bfloat16)

    for s in range(start, stop):
        at = slice(rows * s, rows * (s + 1))
        out = slice(rows * (s - start), rows * (s - start + 1))
        for h in range(heads):
            base = 3 * HD * h
            query = turned[at, base : base + HD]
            keyed = turned[at, base + HD : base + 2 * HD]
            value = turned[at, base + 2 * HD : base + 3 * HD]
            d_ctx = d_context[out, HD * h : HD * (h + 1)]
            ctx = context[at, HD * h : HD * (h + 1)]
            prob = probs[s * heads + h]
            delta = jnp.sum(d_ctx.astype(jnp.float32) * ctx.astype(jnp.float32), -1, keepdims=True)
            d_prob = matmul(d_ctx, value, 1, 1)
            d_score = (prob * (d_prob - delta)).astype(jnp.bfloat16)
            d_query = jnp.dot(d_score, keyed, preferred_element_type=jnp.float32) * scale
            d_key = matmul(d_score, query, 0, 0) * scale
            pair = rotate_back(
                jnp.concatenate([d_query, d_key], axis=1), cosine[at, :], low[at, :], high[at, :]
            )
            d_packed[out, base : base + 2 * HD] = pair
            d_packed[out, base + 2 * HD : base + 3 * HD] = matmul(prob.astype(jnp.bfloat16), d_ctx, 0, 0)
    qkv_grad[...] = jnp.sum(d_packed[...], 0, keepdims=True)
    d_packed_b[...] = d_packed[...].astype(jnp.bfloat16)


def norm_back_body(m, scal, *refs):
    xs = refs[:m]
    cot, head_half, tail_half, weight, slope, inner, vec = refs[m : m + 7]
    outs, five = refs[m + 7 : 2 * m + 7], refs[2 * m + 7]
    rows, width = xs[0].shape
    sums = [jnp.zeros((1, width), jnp.float32) for _ in range(4)]
    for s in range(m):
        at = slice(rows * s, rows * (s + 1))
        half, row = (head_half, rows * s) if s < m // 2 else (tail_half, rows * (s - m // 2))
        d_one = matmul(half[row : row + rows, :], weight[...], 1, 1)
        d_two = matmul(slope[at, :], inner[...], 1, 1)
        xhat, _ = standardize(xs[s][...].astype(jnp.float32))
        for i, part in enumerate((d_one * xhat, d_one, d_two * xhat, d_two)):
            sums[i] = sums[i] + jnp.sum(part, 0, keepdims=True)
        outs[s][...] = (d_one * vec[0:1, :] + d_two * vec[2:3, :]).astype(outs[s].dtype)
    own = jnp.sum(cot[:rows, :].astype(jnp.float32), 0, keepdims=True)
    five[...] = jnp.concatenate([own] + sums + [jnp.zeros((3, width), jnp.float32)], axis=0)


def rest_body(sizes, scal, first, head_half, tail_half, head_grad, tail_grad, inner_grad, *refs):
    strip, qkv_cols, heads = sizes
    five, keep, send, d_packed_b = refs
    count = head_half.shape[0]
    d_packed_b[:count, :] = head_half[...]
    d_packed_b[count:, :] = tail_half[...]
    qkv_grad = head_grad[...] + tail_grad[...]
    pairs = destinations(scal, keep, send)
    for pair in pairs:
        grad = matmul(two_blocks(first, pair, strip), d_packed_b[...], 0, 0).astype(jnp.bfloat16)
        for j, (unused_result, place) in enumerate(pair):
            place[:, :qkv_cols] = grad[strip * j : strip * (j + 1)]
    rows = [[], [], [], []]
    for h in range(heads):
        at = 3 * HD * h
        rows[0].append(qkv_grad[:, at : at + strip])
        rows[1].append(
            jnp.concatenate(
                [qkv_grad[:, at + strip : at + 3 * HD], jnp.zeros((1, 2 * strip - 3 * HD), jnp.float32)], axis=1
            )
        )
        rows[2].append(inner_grad[:, 2 * strip * h : 2 * strip * h + strip])
        rows[3].append(inner_grad[:, 2 * strip * h + strip : 2 * strip * (h + 1)])
    tail = jnp.concatenate(sum(rows, []) + [jnp.zeros((strip - 8 - 4 * heads, strip), jnp.float32)], axis=0)
    for k, place in sum(pairs, []):
        five_k = five[0:8, pl.ds(pl.multiple_of(k * strip, strip), strip)]
        place[:, qkv_cols : qkv_cols + strip] = jnp.concatenate([five_k, tail], axis=0).astype(jnp.bfloat16)


def five_body(scal, *refs):
    parts, outs = refs[:-5], refs[-5:]
    total = parts[0][...]
    for part in parts[1:]:
        total = total + part[...]
    for k, out in enumerate(outs):
        out[...] = total[k : k + 1]


def finish_body(m, scal, *refs):
    x, g = refs[0], refs[1]
    parts = refs[2 : 2 + m]
    (grad,) = refs[2 + m :]
    xhat, scale = standardize(x[...].astype(jnp.float32))
    total = parts[0][...].astype(jnp.float32)
    for part in parts[1:]:
        total = total + part[...].astype(jnp.float32)
    grad[...] = (
        g[...].astype(jnp.float32)
        + scale * (total - jnp.mean(total, -1, keepdims=True) - xhat * jnp.mean(total * xhat, -1, keepdims=True))
    ).astype(grad.dtype)


def pair_shards(
    layer_input,
    out_grad,
    segments,
    positions,
    qkv_weight,
    qkv_bias,
    dense_weight,
    dense_bias,
    inner_weight,
    inner_bias,
    outer_weight,
    outer_bias,
    attention_norm_gain,
    attention_norm_bias,
    feedforward_norm_gain,
    feedforward_norm_bias,
):
    n = lax.axis_size(FSDP)
    m = lax.axis_size(TENSOR)
    f = lax.axis_index(FSDP)
    t = lax.axis_index(TENSOR)
    x = layer_input[0]
    g = out_grad[0]
    rows, width = x.shape
    strip = width // n
    heads = qkv_bias.shape[0]
    wide = heads * HD
    qkv_cols = qkv_weight.shape[1]
    units = inner_weight.shape[1]
    lanes = attention_norm_gain.shape[0]

    bf, fl = jnp.bfloat16, jnp.float32
    masks = slot_masks()
    slot_to_block = [f ^ masks[s] for s in range(8)]
    scal = jnp.stack(slot_to_block + [t, f]).astype(jnp.int32)

    second_msg, x_own, g_own = pl.pallas_call(
        pack_body,
        out_shape=[pltpu.VMEM((strip, 2 * units + wide), bf), pltpu.VMEM(x.shape, bf), pltpu.VMEM(x.shape, bf)],
    )(inner_weight, outer_weight, dense_weight, x, g)
    x_slots = [x_own] + depth_gather(x)[1:]
    as_row = lambda v: v.reshape(1, lanes)
    vectors = (
        attention_norm_gain, attention_norm_bias, feedforward_norm_gain, feedforward_norm_bias, dense_bias, outer_bias
    )
    (first_msg,) = call(
        pack_attend_body,
        [((strip, qkv_cols + strip), bf)],
        [scal, *[as_row(v) for v in vectors], qkv_weight, qkv_bias, inner_bias],
        loose=True,
    )
    second_blocks = gather_blocks(second_msg)
    first_blocks = gather_blocks(first_msg)
    (share,) = call(functools.partial(share_body, qkv_cols), [((8, 16, strip), bf)], [scal, *first_blocks])
    shares = [depth_swap(share, k) for k in range(1, m)]
    g_slots = [g_own] + depth_gather(g)[1:]
    poss = jnp.concatenate([lax.dynamic_slice_in_dim(positions[0], t ^ k, 1, 0) for k in range(m)])
    tables = turn_tables(poss.reshape(m * rows, 1))
    segs = segments[0]
    tokens = m * rows
    sizes = (strip, qkv_cols)
    first, second, turned, probs, context, qkv_w, vec, inner_b = call(
        functools.partial(attend_body, m, heads, sizes),
        [
            ((tokens, width), bf),
            ((tokens, width), bf),
            ((tokens, qkv_cols), bf),
            ((m * heads, rows, rows), fl),
            ((tokens, wide), bf),
            ((width, qkv_cols), bf),
            ((8, width), fl),
            ((1, units), fl),
        ],
        [scal, *x_slots, *first_blocks, *shares, segs, *tables],
        [pltpu.VMEM((8, 16, strip), fl)],
    )
    inner_w, outer_w, dense_w, bend, act, *partial = call(
        functools.partial(feed_body, m, (strip, units, wide)),
        [((width, units), bf), ((units, width), bf), ((wide, width), bf), ((tokens, units), fl), ((tokens, units), bf)]
        + [((rows, width), bf)] * m,
        [scal, second, context, inner_b, *second_blocks],
    )
    mixed = depth_scatter(partial)
    big_keep, big_send, slope, inner_grad, cot = call(
        functools.partial(feed_back_body, m, (strip, units, wide)),
        [
            ((4, strip, 2 * units + wide), bf),
            ((4, strip, 2 * units + wide), bf),
            ((tokens, units), bf),
            ((1, units), fl),
            ((tokens, width), bf),
        ],
        [scal, *g_slots, act, bend, second, context, outer_w],
    )
    big = scatter_sum(big_keep, big_send)
    halves, grads = [], []
    for start, stop in ((0, m // 2), (m // 2, m)):
        half, part = call(
            functools.partial(attend_back_body, start, stop, heads),
            [((rows * (stop - start), qkv_cols), bf), ((1, qkv_cols), fl)],
            [scal, cot, context, dense_w, turned, probs, *tables],
            [pltpu.VMEM((rows * (stop - start), qkv_cols), fl), pltpu.VMEM((rows * (stop - start), wide), bf)],
        )
        halves.append(half)
        grads.append(part)
    *norms, five = call(
        functools.partial(norm_back_body, m),
        [((rows, width), bf)] * m + [((8, width), fl)],
        [scal, *x_slots, cot, *halves, qkv_w, slope, inner_w, vec],
    )
    rest_keep, rest_send = call(
        functools.partial(rest_body, (strip, qkv_cols, heads)),
        [((4, strip, qkv_cols + strip), bf)] * 2,
        [scal, first, *halves, *grads, inner_grad, five],
        [pltpu.VMEM((tokens, qkv_cols), bf)],
    )
    arrived = depth_scatter(norms)
    rest = scatter_sum(rest_keep, rest_send)
    (result,) = call(
        functools.partial(result_body, len(mixed)), [((rows, width), bf)], [scal, x_own, vec, *mixed], final=True
    )
    s_inner, s_outer, s_dense = call(
        functools.partial(unpack_big_body, units, wide),
        [((strip, units), fl), ((units, strip), fl), ((wide, strip), fl)],
        [scal, *big],
        final=True,
    )
    s_qkv, s_qkv_b, s_inner_b, *fives = call(
        functools.partial(unpack_rest_body, (strip, qkv_cols, heads, lanes)),
        [((strip, qkv_cols), fl), (qkv_bias.shape, fl), (inner_bias.shape, fl)] + [((8, lanes), fl)] * m,
        [scal, *rest],
        final=True,
    )
    (in_grad,) = call(
        functools.partial(finish_body, len(arrived)), [((rows, width), bf)], [scal, x_own, g_own, *arrived], final=True
    )
    fives = [fives[0]] + [depth_swap(fives[k], k) for k in range(1, m)]
    five = call(five_body, [((1, lanes), fl)] * 5, [scal, *fives], final=True)
    five = [v.reshape(lanes) for v in five]
    return (
        result[None],
        in_grad[None],
        s_qkv,
        s_qkv_b,
        s_dense,
        five[0],
        s_inner,
        s_inner_b,
        s_outer,
        five[0],
        five[1],
        five[2],
        five[3],
        five[4],
    )


def solution(mesh):
    n, m = mesh.shape[FSDP], mesh.shape[TENSOR]
    paired = n == 8 and m == 4
    shards = plain_shards
    if paired:

        def shards(*args):
            return pair_shards(*args)

    placed = (
        P(None, (FSDP, TENSOR), None),
        P(None, (FSDP, TENSOR), None),
        P(None, FSDP, None),
        P(None, FSDP, None),
        P(FSDP, TENSOR),
        P(TENSOR, FSDP),
        P(TENSOR, FSDP),
        P((FSDP, TENSOR)),
        P(FSDP, TENSOR),
        P(TENSOR, FSDP),
        P(TENSOR, FSDP),
        P((FSDP, TENSOR)),
        P((FSDP, TENSOR)),
        P((FSDP, TENSOR)),
        P((FSDP, TENSOR)),
        P((FSDP, TENSOR)),
    )
    return jax.shard_map(
        shards,
        mesh=mesh,
        in_specs=placed,
        out_specs=(
            P(None, (FSDP, TENSOR), None),
            P(None, (FSDP, TENSOR), None),
            P(FSDP, TENSOR),
            P(TENSOR, FSDP),
            P(TENSOR, FSDP),
            P((FSDP, TENSOR)),
            P(FSDP, TENSOR),
            P(TENSOR, FSDP),
            P(TENSOR, FSDP),
            P((FSDP, TENSOR)),
            P((FSDP, TENSOR)),
            P((FSDP, TENSOR)),
            P((FSDP, TENSOR)),
            P((FSDP, TENSOR)),
        ),
        check_vma=False,
    )
```

```python
import functools

import jax
import jax.numpy as jnp
from jax import lax
from jax.experimental import pallas as pl
from jax.experimental.pallas import tpu as pltpu
from jax.sharding import PartitionSpec as P

H = 16
HD = 64
ROT = 16
FF = 4096


EPS = 1e-05
ROOT_HALF = 0.7071067811865476
INV_ROOT_TAU = 0.3989422804014327
MASKED = -1e30
UNROLL = True
FSDP = "fsdp"
TENSOR = "tensor"
VMEM_LIMIT = 18 * 1024 * 1024


def normalize_rows(token_row_block):
    values = token_row_block.astype(jnp.float32)
    centre = values - jnp.mean(values, -1, keepdims=True)
    scale = lax.rsqrt(jnp.mean(centre * centre, -1, keepdims=True) + EPS)
    return (centre * scale, scale)


def gelu_value(pre):
    return 0.5 * pre * (1.0 + lax.erf(pre * ROOT_HALF))


def gelu_slope(pre):
    return 0.5 * (1.0 + lax.erf(pre * ROOT_HALF)) + pre * jnp.exp(-0.5 * pre * pre) * INV_ROOT_TAU


def angle_tables(positions):
    half = ROT // 2
    freq = jnp.power(10000.0, -jnp.arange(half, dtype=jnp.float32) * (2.0 / ROT))
    angle = positions.astype(jnp.float32)[..., None] * freq
    cosine = jnp.cos(angle)
    sine = jnp.sin(angle)
    return (
        jnp.concatenate([cosine, cosine], -1)[:, :, None, :],
        jnp.concatenate([sine, sine], -1)[:, :, None, :],
    )


def turn(vec, cosine, sine):
    half = ROT // 2
    head = vec[..., :ROT]
    swapped = jnp.concatenate([-head[..., half:], head[..., :half]], -1)
    return jnp.concatenate([head * cosine + swapped * sine, vec[..., ROT:]], -1)


def turn_back(grad, cosine, sine):
    half = ROT // 2
    head = grad[..., :ROT]
    scaled = head * sine
    back = jnp.concatenate([scaled[..., half:], -scaled[..., :half]], -1)
    return jnp.concatenate([head * cosine + back, grad[..., ROT:]], -1)


def attention_mask(segs):
    index = jnp.arange(segs.shape[-1])
    causal = index[None, :, None] >= index[None, None, :]
    return (segs[:, :, None] == segs[:, None, :]) & causal


def matmul(left, right, left_dim, right_dim):
    return lax.dot_general(
        left, right, (((left_dim,), (right_dim,)), ((), ())), preferred_element_type=jnp.float32
    )


def unpack(gathered):
    qkv_w, qkv_b, dense_w, inner_w, inner_b, outer_w = gathered
    return (
        qkv_w,
        qkv_b.reshape(-1).astype(jnp.float32),
        dense_w,
        inner_w,
        inner_b.reshape(-1).astype(jnp.float32),
        outer_w,
    )


def raw_scores(query, keyed, mask, scale):
    product = jnp.einsum("sqhd,skhd->shqk", query, keyed, preferred_element_type=jnp.float32)
    return jnp.where(mask, product * scale, MASKED)


def plain_shards(
    layer_input,
    out_grad,
    segments,
    positions,
    qkv_weight,
    qkv_bias,
    dense_weight,
    dense_bias,
    inner_weight,
    inner_bias,
    outer_weight,
    outer_bias,
    attention_norm_gain,
    attention_norm_bias,
    feedforward_norm_gain,
    feedforward_norm_bias,
):
    attention_gain, attention_bias, feedforward_gain, feedforward_bias, bias_dense, bias_outer = (
        lax.all_gather(attention_norm_gain, (FSDP, TENSOR), axis=0, tiled=True),
        lax.all_gather(attention_norm_bias, (FSDP, TENSOR), axis=0, tiled=True),
        lax.all_gather(feedforward_norm_gain, (FSDP, TENSOR), axis=0, tiled=True),
        lax.all_gather(feedforward_norm_bias, (FSDP, TENSOR), axis=0, tiled=True),
        lax.all_gather(dense_bias, (FSDP, TENSOR), axis=0, tiled=True),
        lax.all_gather(outer_bias, (FSDP, TENSOR), axis=0, tiled=True),
    )
    scale = HD ** (-0.5)
    microbatch = 0
    weights = unpack(
        (
            lax.all_gather(qkv_weight, FSDP, axis=0, tiled=True),
            lax.all_gather(qkv_bias, FSDP, axis=1, tiled=True),
            lax.all_gather(dense_weight, FSDP, axis=1, tiled=True),
            lax.all_gather(inner_weight, FSDP, axis=0, tiled=True),
            lax.all_gather(inner_bias, FSDP, axis=1, tiled=True),
            lax.all_gather(outer_weight, FSDP, axis=1, tiled=True),
        )
    )
    qkv_w, qkv_b, dense_w, inner_w, inner_b, outer_w = weights
    token_row_block = lax.all_gather(layer_input[microbatch], TENSOR, axis=0, tiled=True)
    segs = segments[microbatch]
    seqs, length = segs.shape
    heads = qkv_w.shape[1] // (3 * HD)
    normalized_input, _ = normalize_rows(token_row_block)
    first_branch = (normalized_input * attention_gain + attention_bias).astype(jnp.bfloat16)
    second_branch = (normalized_input * feedforward_gain + feedforward_bias).astype(jnp.bfloat16)
    packed = (jnp.dot(first_branch, qkv_w, preferred_element_type=jnp.float32) + qkv_b).reshape(
        seqs, length, heads, 3, HD
    )
    cosine, sine = angle_tables(positions[microbatch])
    query = turn(packed[:, :, :, 0], cosine, sine).astype(jnp.bfloat16)
    keyed = turn(packed[:, :, :, 1], cosine, sine).astype(jnp.bfloat16)
    value = packed[:, :, :, 2].astype(jnp.bfloat16)
    mask = attention_mask(segs)[:, None]
    scores = raw_scores(query, keyed, mask, scale)
    peak = jnp.max(scores, -1, keepdims=True)
    log_total = peak + jnp.log(jnp.sum(jnp.exp(scores - peak), -1, keepdims=True))
    probs_b = jnp.exp(scores - log_total).astype(jnp.bfloat16)
    context = jnp.einsum(
        "shqk,skhd->sqhd", probs_b, value, preferred_element_type=jnp.float32
    ).astype(jnp.bfloat16)
    flat_ctx = context.reshape(seqs * length, heads * HD)
    pre = jnp.dot(second_branch, inner_w, preferred_element_type=jnp.float32) + inner_b
    act = gelu_value(pre).astype(jnp.bfloat16)
    ctx_rows = flat_ctx
    act_rows = act
    mixed = lax.psum_scatter(
        (
            jnp.dot(ctx_rows, dense_w, preferred_element_type=jnp.float32)
            + jnp.dot(act_rows, outer_w, preferred_element_type=jnp.float32)
        ).astype(jnp.bfloat16),
        TENSOR,
        scatter_dimension=0,
        tiled=True,
    ).astype(jnp.float32)
    outputs = [
        (layer_input[microbatch].astype(jnp.float32) + mixed + bias_dense + bias_outer).astype(
            jnp.bfloat16
        )
    ]
    saved = [
        (
            token_row_block,
            first_branch,
            second_branch,
            query,
            keyed,
            value,
            log_total,
            context,
            flat_ctx,
            pre,
            act,
        )
    ]
    g_qkv_b = jnp.zeros((qkv_bias.shape[0], 3 * HD), jnp.float32)
    g_inner_b = jnp.zeros((inner_bias.shape[0], FF // H), jnp.float32)
    microbatch = 0
    weights = unpack(
        (
            lax.all_gather(qkv_weight, FSDP, axis=0, tiled=True),
            lax.all_gather(qkv_bias, FSDP, axis=1, tiled=True),
            lax.all_gather(dense_weight, FSDP, axis=1, tiled=True),
            lax.all_gather(inner_weight, FSDP, axis=0, tiled=True),
            lax.all_gather(inner_bias, FSDP, axis=1, tiled=True),
            lax.all_gather(outer_weight, FSDP, axis=1, tiled=True),
        )
    )
    qkv_w, qkv_b, dense_w, inner_w, inner_b, outer_w = weights
    (
        token_row_block,
        first_branch,
        second_branch,
        query,
        keyed,
        value,
        log_total,
        context,
        flat_ctx,
        pre,
        act,
    ) = saved[microbatch]
    segs = segments[microbatch]
    seqs, length = segs.shape
    heads = qkv_w.shape[1] // (3 * HD)
    cot_rows = lax.all_gather(out_grad[microbatch], TENSOR, axis=0, tiled=True)
    own_cot = out_grad[microbatch].astype(jnp.float32)
    g_bias = jnp.sum(own_cot, 0)
    d_act = matmul(cot_rows, outer_w, 1, 1)
    g_outer = matmul(act, cot_rows, 0, 0)
    d_pre = d_act * gelu_slope(pre)
    g_inner_b = jnp.sum(d_pre, 0).reshape(g_inner_b.shape)
    d_pre_b = d_pre.astype(jnp.bfloat16)
    g_inner = matmul(second_branch, d_pre_b, 0, 0)
    second_branch_gradient = matmul(d_pre_b, inner_w, 1, 1)
    d_ctx = matmul(cot_rows, dense_w, 1, 1).astype(jnp.bfloat16)
    g_dense = matmul(flat_ctx, cot_rows, 0, 0)
    d_ctx4 = d_ctx.reshape(context.shape)
    delta = jnp.sum(d_ctx4.astype(jnp.float32) * context.astype(jnp.float32), -1)
    mask = attention_mask(segs)[:, None]
    probs = jnp.exp(raw_scores(query, keyed, mask, scale) - log_total)
    d_probs = jnp.einsum("sqhd,skhd->shqk", d_ctx4, value, preferred_element_type=jnp.float32)
    d_scores = probs * (d_probs - jnp.transpose(delta, (0, 2, 1))[..., None])
    d_value = jnp.einsum(
        "shqk,sqhd->skhd", probs.astype(jnp.bfloat16), d_ctx4, preferred_element_type=jnp.float32
    )
    d_scores_b = d_scores.astype(jnp.bfloat16)
    d_query = (
        jnp.einsum("shqk,skhd->sqhd", d_scores_b, keyed, preferred_element_type=jnp.float32) * scale
    )
    d_key = (
        jnp.einsum("shqk,sqhd->skhd", d_scores_b, query, preferred_element_type=jnp.float32) * scale
    )
    cosine, sine = angle_tables(positions[microbatch])
    d_packed = jnp.stack(
        [turn_back(d_query, cosine, sine), turn_back(d_key, cosine, sine), d_value], 3
    )
    d_packed = d_packed.reshape(seqs * length, heads * 3 * HD)
    g_qkv_b = jnp.sum(d_packed, 0).reshape(g_qkv_b.shape)
    d_packed_b = d_packed.astype(jnp.bfloat16)
    g_qkv = matmul(first_branch, d_packed_b, 0, 0)
    first_branch_gradient = matmul(d_packed_b, qkv_w, 1, 1)
    local_normalized_input, local_inverse_deviation = normalize_rows(layer_input[microbatch])
    local_first_branch = lax.psum_scatter(
        first_branch_gradient.astype(jnp.bfloat16), TENSOR, scatter_dimension=0, tiled=True
    ).astype(jnp.float32)
    local_second_branch = lax.psum_scatter(
        second_branch_gradient.astype(jnp.bfloat16), TENSOR, scatter_dimension=0, tiled=True
    ).astype(jnp.float32)
    attention_gain_gradient = jnp.sum(local_first_branch * local_normalized_input, 0)
    g_shift1 = jnp.sum(local_first_branch, 0)
    feedforward_gain_gradient = jnp.sum(local_second_branch * local_normalized_input, 0)
    g_shift2 = jnp.sum(local_second_branch, 0)
    normalized_gradient = (
        local_first_branch * attention_gain + local_second_branch * feedforward_gain
    )
    input_gradient = own_cot + local_inverse_deviation * (
        normalized_gradient
        - jnp.mean(normalized_gradient, -1, keepdims=True)
        - local_normalized_input
        * jnp.mean(normalized_gradient * local_normalized_input, -1, keepdims=True)
    )
    in_grads = [input_gradient.astype(jnp.bfloat16)]
    s_qkv, s_qkv_b, s_dense, s_inner, s_inner_b, s_outer = (
        lax.psum_scatter(
            g_qkv.astype(jnp.bfloat16), FSDP, scatter_dimension=0, tiled=True
        ).astype(jnp.float32),
        lax.psum_scatter(
            g_qkv_b.astype(jnp.bfloat16), FSDP, scatter_dimension=1, tiled=True
        ).astype(jnp.float32),
        lax.psum_scatter(
            g_dense.astype(jnp.bfloat16), FSDP, scatter_dimension=1, tiled=True
        ).astype(jnp.float32),
        lax.psum_scatter(
            g_inner.astype(jnp.bfloat16), FSDP, scatter_dimension=0, tiled=True
        ).astype(jnp.float32),
        lax.psum_scatter(
            g_inner_b.astype(jnp.bfloat16), FSDP, scatter_dimension=1, tiled=True
        ).astype(jnp.float32),
        lax.psum_scatter(
            g_outer.astype(jnp.bfloat16), FSDP, scatter_dimension=1, tiled=True
        ).astype(jnp.float32),
    )
    s_bias, s_gain1, s_shift1, s_gain2, s_shift2 = (
        lax.psum_scatter(g_bias, (FSDP, TENSOR), scatter_dimension=0, tiled=True),
        lax.psum_scatter(
            attention_gain_gradient, (FSDP, TENSOR), scatter_dimension=0, tiled=True
        ),
        lax.psum_scatter(g_shift1, (FSDP, TENSOR), scatter_dimension=0, tiled=True),
        lax.psum_scatter(
            feedforward_gain_gradient, (FSDP, TENSOR), scatter_dimension=0, tiled=True
        ),
        lax.psum_scatter(g_shift2, (FSDP, TENSOR), scatter_dimension=0, tiled=True),
    )
    return (
        jnp.stack(outputs),
        jnp.stack(in_grads),
        s_qkv,
        s_qkv_b,
        s_dense,
        s_bias,
        s_inner,
        s_inner_b,
        s_outer,
        s_bias,
        s_gain1,
        s_shift1,
        s_gain2,
        s_shift2,
    )


def swap(value, axis, partner):
    count = lax.axis_size(axis)
    return lax.ppermute(value, axis, [(i, partner(i)) for i in range(count)])


def core_swap(value):
    return swap(value, FSDP, lambda i: i ^ 1)


def near_swap(value):
    return swap(value, FSDP, lambda i: i ^ (4 if i & 1 else 2))


def far_swap(value):
    return swap(value, FSDP, lambda i: i ^ (2 if i & 1 else 4))


def depth_swap(value, mask):
    return swap(value, TENSOR, lambda i: i ^ mask)


def depth_gather(value):
    second = depth_swap(value, 2)
    first = depth_swap(value, 1)
    return [value, first, second, depth_swap(second, 1)]


def depth_scatter(parts):
    third = depth_swap(parts[3], 1)
    first = depth_swap(parts[1], 1)
    (second,) = call(
        one_sum_body, [(third.shape, jnp.bfloat16)], [jnp.zeros((1,), jnp.int32), parts[2], third]
    )
    return [parts[0], first, depth_swap(second, 2)]


def slot_masks():
    core = lax.axis_index(FSDP) & 1
    near = jnp.where(core == 0, 2, 4)
    far = 6 - near
    return [0, 1, near, near + 1, far, far + 1, 6, 7]


def gather_blocks(shard):
    partner = core_swap(shard)
    near_own = near_swap(shard)
    near_partner = near_swap(partner)
    across = far_swap(near_own)
    far_partner = core_swap(near_own)
    far_own = core_swap(near_partner)
    across_partner = core_swap(across)
    return [shard, partner, near_own, near_partner, far_own, far_partner, across, across_partner]


def scatter_sum(keep, send):
    shape = keep.shape[1:]
    got = core_swap(send)
    own, near_own, near_partner, across = call(
        four_sums_body, [(shape, jnp.bfloat16)] * 4, [jnp.zeros((1,), jnp.int32), keep, got]
    )
    across = far_swap(across)
    near_partner = near_swap(near_partner)
    (near_own,) = call(one_sum_body, [(shape, jnp.bfloat16)], [jnp.zeros((1,), jnp.int32), near_own, across])
    near_own = near_swap(near_own)
    far = core_swap(near_partner)
    return [own, near_own, far]


def turn_tables(positions):
    half = ROT // 2
    lane = jnp.arange(2 * HD) % HD
    freq = jnp.power(10000.0, -(lane % half).astype(jnp.float32) * (2.0 / ROT))
    angle = positions.astype(jnp.float32) * freq
    sine = jnp.sin(angle)
    return (
        jnp.where(lane < ROT, jnp.cos(angle), 1.0),
        jnp.where(lane < half, -sine, 0.0),
        jnp.where((lane >= half) & (lane < ROT), sine, 0.0),
    )


def erf_value(value):
    v = jnp.clip(value, -4.0, 4.0)
    s = v * v
    top = jnp.full_like(s, -2.72614225801306e-10)
    for c in (2.77068142495902e-08, -2.10102402082508e-06, -5.69250639462346e-05, -7.34990630326855e-04, -2.95459980854025e-03, -1.60960333262415e-02):
        top = top * s + c
    low = jnp.full_like(s, -1.45660718464996e-05)
    for c in (-2.13374055278905e-04, -1.68282697438203e-03, -7.37332916720468e-03, -1.42647390514189e-02):
        low = low * s + c
    return v * top / low


def call(body, outs, ins, scratch=(), final=False, loose=False):
    specs = [pl.BlockSpec(memory_space=pltpu.SMEM)] + [pl.BlockSpec(memory_space=pltpu.VMEM)] * (len(ins) - 1)
    return pl.pallas_call(
        body,
        out_shape=[jax.ShapeDtypeStruct(*out) if final else pltpu.VMEM(*out) for out in outs],
        in_specs=specs,
        out_specs=[pl.BlockSpec(memory_space=pltpu.VMEM)] * len(outs),
        scratch_shapes=list(scratch),
        compiler_params=pltpu.CompilerParams(vmem_limit_bytes=VMEM_LIMIT),
    )(ins[0], *[pltpu.with_memory_space_constraint(a, pltpu.HBM if loose else pltpu.VMEM) for a in ins[1:]])


def four_sums_body(scal, keep, got, *outs):
    for i, out in enumerate(outs):
        out[...] = (keep[i].astype(jnp.float32) + got[i].astype(jnp.float32)).astype(out.dtype)


def one_sum_body(scal, one, two, out):
    out[...] = (one[...].astype(jnp.float32) + two[...].astype(jnp.float32)).astype(out.dtype)


def pack_body(inner, outer, dense, x, g, segs, message, x_copy, g_copy, segs_copy):
    segs_copy[...] = segs[...]
    x_copy[...] = x[...]
    g_copy[...] = g[...]
    strip, units = inner.shape
    message[:, :units] = inner[...]
    for i in range(outer.shape[0] // strip):
        message[:, units + strip * i : units + strip * (i + 1)] = outer[strip * i : strip * (i + 1), :]
    for i in range(dense.shape[0] // strip):
        message[:, 2 * units + strip * i : 2 * units + strip * (i + 1)] = dense[strip * i : strip * (i + 1), :]


def in_three(value):
    high = value.astype(jnp.bfloat16)
    rest = value - high.astype(jnp.float32)
    middle = rest.astype(jnp.bfloat16)
    return [part.astype(jnp.float32) for part in (high, middle, rest - middle.astype(jnp.float32))]


def placed(value, lanes, shift):
    rows, count = value.shape
    wide = jnp.concatenate([value, jnp.zeros((rows, lanes - count), value.dtype)], axis=1)
    return pltpu.roll(wide, shift, 1)


def pack_attend_body(scal, *refs):
    vectors, qkv, qkv_bias, inner_bias, message = refs[:6], refs[6], refs[7], refs[8], refs[9]
    strip, cols = qkv.shape
    lanes = vectors[0].shape[1]
    rows = [ref[...] for ref in vectors[:4]] + [vectors[4][...] + vectors[5][...]]
    parts = in_three(jnp.concatenate(rows, axis=0))
    three = jnp.concatenate(parts + [jnp.zeros((1, lanes), jnp.float32)], axis=0)
    biases = []
    for ref in (qkv_bias, inner_bias):
        value = placed(ref[...].astype(jnp.float32), 2 * strip, scal[9] * ref.shape[1])
        biases += [value[:, :strip], value[:, strip:]]
    small = jnp.concatenate([placed(three, strip, scal[8] * lanes)] + biases, axis=0)
    message[:, :cols] = qkv[...]
    message[:, cols:] = jnp.concatenate(
        [small, jnp.zeros((strip - small.shape[0], strip), jnp.float32)], axis=0
    ).astype(jnp.bfloat16)


def share_body(cols, scal, *refs):
    blocks, out = refs[:-1], refs[-1]
    for i, block in enumerate(blocks):
        out[i] = block[0:16, cols:]


def unpack_big_body(units, wide, scal, own, near, far, inner, outer, dense):
    total = own[...].astype(jnp.float32) + near[...].astype(jnp.float32) + far[...].astype(jnp.float32)
    strip = total.shape[0]
    inner[...] = total[:, :units]
    for i in range(units // strip):
        outer[strip * i : strip * (i + 1), :] = total[:, units + strip * i : units + strip * (i + 1)]
    for i in range(wide // strip):
        dense[strip * i : strip * (i + 1), :] = total[:, 2 * units + strip * i : 2 * units + strip * (i + 1)]


def unpack_rest_body(scal, own, near, far, qkv):
    qkv[...] = own[...].astype(jnp.float32) + near[...].astype(jnp.float32) + far[...].astype(jnp.float32)


def unpack_small_body(sizes, scal, own, near, far, qkv_b, inner_b, *fives):
    strip, heads, lanes = sizes
    tiny = own[...].astype(jnp.float32) + near[...].astype(jnp.float32) + far[...].astype(jnp.float32)
    for i, out in enumerate((qkv_b, inner_b)):
        at = 8 + 2 * heads * i
        pair = jnp.concatenate([tiny[at : at + heads], tiny[at + heads : at + 2 * heads]], axis=1)
        count = out.shape[1]
        out[...] = pltpu.roll(pair, 2 * strip - scal[9] * count, 1)[:, :count]
    mine = pltpu.roll(tiny[0:8], strip - scal[8] * lanes, 1)[:, :lanes]
    for k, out in enumerate(fives):
        out[...] = mine[k]


def result_body(m, scal, x, vec, *refs):
    total = x[...].astype(jnp.float32) + vec[4:5, :]
    for part in refs[:m]:
        total = total + part[...].astype(jnp.float32)
    refs[m][...] = total.astype(refs[m].dtype)


def standardize(values):
    centre = values - jnp.mean(values, -1, keepdims=True)
    scale = lax.rsqrt(jnp.mean(centre * centre, -1, keepdims=True) + EPS)
    return centre * scale, scale


def rotate(pair, cosine, low, high):
    lanes = pair.shape[-1]
    half = ROT // 2
    return pair * cosine + pltpu.roll(pair, lanes - half, 1) * low + pltpu.roll(pair, half, 1) * high


def rotate_back(pair, cosine, low, high):
    lanes = pair.shape[-1]
    half = ROT // 2
    return pair * cosine - pltpu.roll(pair, lanes - half, 1) * low - pltpu.roll(pair, half, 1) * high


def attend_body(m, heads, sizes, scal, *refs):
    strip, qkv_cols = sizes
    xs, blocks, shares = refs[:m], refs[m : m + 8], refs[m + 8 : 2 * m + 7]
    segs, cosine, low, high = refs[2 * m + 7 : 2 * m + 11]
    first, second, turned, probs, context, weight, vec, inner_b, smalls = refs[2 * m + 11 :]
    count = 8
    biases = jnp.zeros((4 * heads, strip), jnp.float32)
    for slot, view in enumerate(blocks):
        k = scal[slot]
        weight[pl.ds(pl.multiple_of(k * strip, strip), strip), :] = view[:, :qkv_cols]
        biases = biases + view[16 : 16 + 4 * heads, qkv_cols:].astype(jnp.float32)
        part = view[0:16, qkv_cols:].astype(jnp.float32)
        for share in shares:
            part = part + share[slot].astype(jnp.float32)
        smalls[k] = part
    for k in range(count):
        s = smalls[k]
        vec[0:5, strip * k : strip * (k + 1)] = s[0:5] + s[5:10] + s[10:15]
    rest = 3 * HD - strip
    qkv_b = jnp.concatenate(
        [piece for h in range(heads) for piece in (biases[h : h + 1], biases[heads + h : heads + h + 1, :rest])], axis=1
    )
    inner_b[...] = jnp.concatenate(
        [biases[at + h : at + h + 1] for h in range(heads) for at in (2 * heads, 3 * heads)], axis=1
    )
    rows = xs[0].shape[0]
    scale = HD ** (-0.5)
    after = lax.broadcasted_iota(jnp.int32, (rows, rows), 0) >= lax.broadcasted_iota(jnp.int32, (rows, rows), 1)
    for s in range(m):
        at = slice(rows * s, rows * (s + 1))
        xhat, _ = standardize(xs[s][...].astype(jnp.float32))
        one = (xhat * vec[0:1, :] + vec[1:2, :]).astype(jnp.bfloat16)
        first[at, :] = one
        second[at, :] = (xhat * vec[2:3, :] + vec[3:4, :]).astype(jnp.bfloat16)
    packed = jnp.dot(first[...], weight[...], preferred_element_type=jnp.float32) + qkv_b
    cos, lo, hi = cosine[...], low[...], high[...]
    for h in range(heads):
        base = 3 * HD * h
        pair = packed[:, base : base + 2 * HD]
        turned[:, base : base + 2 * HD] = rotate(pair, cos, lo, hi).astype(jnp.bfloat16)
        turned[:, base + 2 * HD : base + 3 * HD] = packed[:, base + 2 * HD : base + 3 * HD].astype(jnp.bfloat16)
    def one_sequence(s, unused):
        at = pl.ds(pl.multiple_of(s * rows, rows), rows)
        seg = jnp.broadcast_to(segs[pl.ds(scal[8] ^ s, 1), :].astype(jnp.float32), (rows, rows))
        mask = (seg == jnp.transpose(seg)) & after
        for h in range(heads):
            base = 3 * HD * h
            query = turned[at, base : base + HD]
            keyed = turned[at, base + HD : base + 2 * HD]
            value = turned[at, base + 2 * HD : base + 3 * HD]
            scores = jnp.where(mask, matmul(query, keyed, 1, 1) * scale, MASKED)
            peak = jnp.max(scores, -1, keepdims=True)
            raised = jnp.exp(scores - peak)
            prob = raised / jnp.sum(raised, -1, keepdims=True)
            probs[s * heads + h] = prob
            context[at, HD * h : HD * (h + 1)] = jnp.dot(
                prob.astype(jnp.bfloat16), value, preferred_element_type=jnp.float32
            ).astype(jnp.bfloat16)
        return unused

    lax.fori_loop(0, m, one_sequence, 0, unroll=UNROLL)


def feed_act_body(m, sizes, scal, *refs):
    strip, units = sizes
    second, inner_b, blocks = refs[0], refs[1], refs[2:10]
    inner, bend, act = refs[10:]
    for slot, view in enumerate(blocks):
        inner[pl.ds(pl.multiple_of(scal[slot] * strip, strip), strip), :] = view[:, :units]
    rows = second.shape[0] // m
    for s in range(m):
        at = slice(rows * s, rows * (s + 1))
        value = jnp.dot(second[at, :], inner[...], preferred_element_type=jnp.float32) + inner_b[...]
        half = 0.5 * (1.0 + erf_value(value * ROOT_HALF))
        act[at, :] = (value * half).astype(jnp.bfloat16)
        bend[at, :] = half + value * jnp.exp(-0.5 * value * value) * INV_ROOT_TAU


def feed_out_body(m, sizes, scal, *refs):
    strip, units, wide = sizes
    act, context, blocks = refs[0], refs[1], refs[2:10]
    outer, dense = refs[10:12]
    outs = refs[12:]
    for slot, view in enumerate(blocks):
        at = pl.ds(pl.multiple_of(scal[slot] * strip, strip), strip)
        for i in range(units // strip):
            outer[strip * i : strip * (i + 1), at] = view[:, units + strip * i : units + strip * (i + 1)]
        for i in range(wide // strip):
            dense[strip * i : strip * (i + 1), at] = view[:, 2 * units + strip * i : 2 * units + strip * (i + 1)]
    rows = outs[0].shape[0]
    for s in range(m):
        at = slice(rows * s, rows * (s + 1))
        mixed = jnp.dot(act[at, :], outer[...], preferred_element_type=jnp.float32)
        mixed = mixed + jnp.dot(context[at, :], dense[...], preferred_element_type=jnp.float32)
        outs[s][...] = mixed.astype(outs[s].dtype)


def destinations(scal, keep, send):
    places = [(scal[slot], keep.at[j]) for j, slot in enumerate((0, 2, 3, 6))]
    places += [(scal[slot], send.at[j]) for j, slot in enumerate((1, 5, 4, 7))]
    return [places[i : i + 2] for i in range(0, len(places), 2)]


def two_blocks(source, pair, strip):
    return jnp.concatenate(
        [source[:, pl.ds(pl.multiple_of(k * strip, strip), strip)] for k, unused_result in pair], axis=1
    )


def feed_back_body(m, sizes, scal, *refs):
    strip, units, wide = sizes
    gs = refs[:m]
    act, bend, second, context, outer = refs[m : m + 5]
    keep, send, slope, g_inner_b, cot = refs[m + 5 :]
    rows = gs[0].shape[0]
    for s in range(m):
        cot[rows * s : rows * (s + 1), :] = gs[s][...]
    pairs = destinations(scal, keep, send)
    for pair in pairs:
        columns = two_blocks(cot, pair, strip)
        for source, count, start in ((act, units, units), (context, wide, 2 * units)):
            grad = matmul(source[...], columns, 0, 0).astype(jnp.bfloat16)
            for j, (unused_result, place) in enumerate(pair):
                for i in range(count // strip):
                    place[:, start + strip * i : start + strip * (i + 1)] = grad[
                        strip * i : strip * (i + 1), strip * j : strip * (j + 1)
                    ]
    total = jnp.zeros((1, units), jnp.float32)
    for s in range(m):
        at = slice(rows * s, rows * (s + 1))
        grad = matmul(cot[at, :], outer[...], 1, 1) * bend[at, :]
        total = total + jnp.sum(grad, 0, keepdims=True)
        slope[at, :] = grad.astype(jnp.bfloat16)
    g_inner_b[...] = total
    for pair in pairs:
        grad = matmul(two_blocks(second, pair, strip), slope[...], 0, 0).astype(jnp.bfloat16)
        for j, (unused_result, place) in enumerate(pair):
            place[:, :units] = grad[strip * j : strip * (j + 1)]


def attend_back_body(start, stop, heads, scal, *refs):
    cot, context, dense, turned, probs, cosine, low, high = refs[:8]
    d_packed_b, qkv_grad, d_packed, d_context = refs[8:]
    rows = d_context.shape[0] // (stop - start)
    scale = HD ** (-0.5)
    d_context[...] = matmul(cot[rows * start : rows * stop, :], dense[...], 1, 1).astype(jnp.bfloat16)

    for s in range(start, stop):
        at = slice(rows * s, rows * (s + 1))
        out = slice(rows * (s - start), rows * (s - start + 1))
        for h in range(heads):
            base = 3 * HD * h
            query = turned[at, base : base + HD]
            keyed = turned[at, base + HD : base + 2 * HD]
            value = turned[at, base + 2 * HD : base + 3 * HD]
            d_ctx = d_context[out, HD * h : HD * (h + 1)]
            ctx = context[at, HD * h : HD * (h + 1)]
            prob = probs[s * heads + h]
            delta = jnp.sum(d_ctx.astype(jnp.float32) * ctx.astype(jnp.float32), -1, keepdims=True)
            d_prob = matmul(d_ctx, value, 1, 1)
            d_score = (prob * (d_prob - delta)).astype(jnp.bfloat16)
            d_query = jnp.dot(d_score, keyed, preferred_element_type=jnp.float32) * scale
            d_key = matmul(d_score, query, 0, 0) * scale
            pair = rotate_back(
                jnp.concatenate([d_query, d_key], axis=1), cosine[at, :], low[at, :], high[at, :]
            )
            d_packed[out, base : base + 2 * HD] = pair
            d_packed[out, base + 2 * HD : base + 3 * HD] = matmul(prob.astype(jnp.bfloat16), d_ctx, 0, 0)
    qkv_grad[...] = jnp.sum(d_packed[...], 0, keepdims=True)
    d_packed_b[...] = d_packed[...].astype(jnp.bfloat16)


def norm_back_body(m, scal, *refs):
    xs = refs[:m]
    cot, head_half, tail_half, weight, slope, inner, vec = refs[m : m + 7]
    outs, five = refs[m + 7 : 2 * m + 7], refs[2 * m + 7]
    rows, width = xs[0].shape
    sums = [jnp.zeros((1, width), jnp.float32) for _ in range(4)]
    for s in range(m):
        at = slice(rows * s, rows * (s + 1))
        half, row = (head_half, rows * s) if s < m // 2 else (tail_half, rows * (s - m // 2))
        d_one = matmul(half[row : row + rows, :], weight[...], 1, 1)
        d_two = matmul(slope[at, :], inner[...], 1, 1)
        xhat, _ = standardize(xs[s][...].astype(jnp.float32))
        for i, part in enumerate((d_one * xhat, d_one, d_two * xhat, d_two)):
            sums[i] = sums[i] + jnp.sum(part, 0, keepdims=True)
        outs[s][...] = (d_one * vec[0:1, :] + d_two * vec[2:3, :]).astype(outs[s].dtype)
    own = jnp.sum(cot[:rows, :].astype(jnp.float32), 0, keepdims=True)
    five[...] = jnp.concatenate([own] + sums + [jnp.zeros((3, width), jnp.float32)], axis=0)


def rest_body(strip, scal, first, head_half, tail_half, keep, send, d_packed_b):
    count = head_half.shape[0]
    d_packed_b[:count, :] = head_half[...]
    d_packed_b[count:, :] = tail_half[...]
    for pair in destinations(scal, keep, send):
        grad = matmul(two_blocks(first, pair, strip), d_packed_b[...], 0, 0).astype(jnp.bfloat16)
        for j, (unused_result, place) in enumerate(pair):
            place[...] = grad[strip * j : strip * (j + 1)]


def small_body(sizes, scal, head_grad, tail_grad, inner_grad, *refs):
    strip, heads = sizes
    fives, (keep, send, five) = refs[:-3], refs[-3:]
    total = fives[0][...]
    for part in fives[1:]:
        total = total + part[...]
    five[...] = total
    qkv_grad = head_grad[...] + tail_grad[...]
    rows = [[], [], [], []]
    for h in range(heads):
        at = 3 * HD * h
        rows[0].append(qkv_grad[:, at : at + strip])
        rows[1].append(
            jnp.concatenate(
                [qkv_grad[:, at + strip : at + 3 * HD], jnp.zeros((1, 2 * strip - 3 * HD), jnp.float32)], axis=1
            )
        )
        rows[2].append(inner_grad[:, 2 * strip * h : 2 * strip * h + strip])
        rows[3].append(inner_grad[:, 2 * strip * h + strip : 2 * strip * (h + 1)])
    spare = keep.shape[1] - 8 - 4 * heads
    tail = jnp.concatenate(sum(rows, []) + [jnp.zeros((spare, strip), jnp.float32)], axis=0)
    for k, place in sum(destinations(scal, keep, send), []):
        five_k = five[0:8, pl.ds(pl.multiple_of(k * strip, strip), strip)]
        place[...] = jnp.concatenate([five_k, tail], axis=0).astype(jnp.bfloat16)


def finish_body(m, scal, *refs):
    x, g = refs[0], refs[1]
    parts = refs[2 : 2 + m]
    (grad,) = refs[2 + m :]
    xhat, scale = standardize(x[...].astype(jnp.float32))
    total = parts[0][...].astype(jnp.float32)
    for part in parts[1:]:
        total = total + part[...].astype(jnp.float32)
    grad[...] = (
        g[...].astype(jnp.float32)
        + scale * (total - jnp.mean(total, -1, keepdims=True) - xhat * jnp.mean(total * xhat, -1, keepdims=True))
    ).astype(grad.dtype)


def pair_shards(
    layer_input,
    out_grad,
    segments,
    positions,
    qkv_weight,
    qkv_bias,
    dense_weight,
    dense_bias,
    inner_weight,
    inner_bias,
    outer_weight,
    outer_bias,
    attention_norm_gain,
    attention_norm_bias,
    feedforward_norm_gain,
    feedforward_norm_bias,
):
    n = lax.axis_size(FSDP)
    m = lax.axis_size(TENSOR)
    f = lax.axis_index(FSDP)
    t = lax.axis_index(TENSOR)
    x = layer_input[0]
    g = out_grad[0]
    rows, width = x.shape
    strip = width // n
    heads = qkv_bias.shape[0]
    wide = heads * HD
    qkv_cols = qkv_weight.shape[1]
    units = inner_weight.shape[1]
    lanes = attention_norm_gain.shape[0]

    bf, fl = jnp.bfloat16, jnp.float32
    masks = slot_masks()
    slot_to_block = [f ^ masks[s] for s in range(8)]
    scal = jnp.stack(slot_to_block + [t, f]).astype(jnp.int32)

    second_msg, x_own, g_own, segs = pl.pallas_call(
        pack_body,
        out_shape=[pltpu.VMEM((strip, 2 * units + wide), bf), pltpu.VMEM(x.shape, bf), pltpu.VMEM(x.shape, bf), pltpu.VMEM(segments.shape[1:], jnp.int32)],
    )(inner_weight, outer_weight, dense_weight, x, g, segments[0])
    x_slots = [x_own] + depth_gather(x)[1:]
    as_row = lambda v: v.reshape(1, lanes)
    vectors = (
        attention_norm_gain, attention_norm_bias, feedforward_norm_gain, feedforward_norm_bias, dense_bias, outer_bias
    )
    (first_msg,) = call(
        pack_attend_body,
        [((strip, qkv_cols + strip), bf)],
        [scal, *[as_row(v) for v in vectors], qkv_weight, qkv_bias, inner_bias],
        loose=True,
    )
    second_blocks = gather_blocks(second_msg)
    first_blocks = gather_blocks(first_msg)
    (share,) = call(functools.partial(share_body, qkv_cols), [((8, 16, strip), bf)], [scal, *first_blocks])
    shares = [depth_swap(share, k) for k in range(1, m)]
    g_slots = [g_own] + depth_gather(g)[1:]
    poss = jnp.concatenate([lax.dynamic_slice_in_dim(positions[0], t ^ k, 1, 0) for k in range(m)])
    tables = turn_tables(poss.reshape(m * rows, 1))
    tokens = m * rows
    sizes = (strip, qkv_cols)
    first, second, turned, probs, context, qkv_w, vec, inner_b = call(
        functools.partial(attend_body, m, heads, sizes),
        [
            ((tokens, width), bf),
            ((tokens, width), bf),
            ((tokens, qkv_cols), bf),
            ((m * heads, rows, rows), fl),
            ((tokens, wide), bf),
            ((width, qkv_cols), bf),
            ((8, width), fl),
            ((1, units), fl),
        ],
        [scal, *x_slots, *first_blocks, *shares, segs, *tables],
        [pltpu.VMEM((8, 16, strip), fl)],
    )
    inner_w, bend, act = call(
        functools.partial(feed_act_body, m, (strip, units)),
        [((width, units), bf), ((tokens, units), fl), ((tokens, units), bf)],
        [scal, second, inner_b, *second_blocks],
    )
    outer_w, dense_w, *partial = call(
        functools.partial(feed_out_body, m, (strip, units, wide)),
        [((units, width), bf), ((wide, width), bf)] + [((rows, width), bf)] * m,
        [scal, act, context, *second_blocks],
    )
    mixed = [partial[0]] + [depth_swap(partial[k], k) for k in range(1, m)]
    big_keep, big_send, slope, inner_grad, cot = call(
        functools.partial(feed_back_body, m, (strip, units, wide)),
        [
            ((4, strip, 2 * units + wide), bf),
            ((4, strip, 2 * units + wide), bf),
            ((tokens, units), bf),
            ((1, units), fl),
            ((tokens, width), bf),
        ],
        [scal, *g_slots, act, bend, second, context, outer_w],
    )
    big = scatter_sum(big_keep, big_send)
    halves, grads = [], []
    for start, stop in ((0, m // 2), (m // 2, m)):
        half, part = call(
            functools.partial(attend_back_body, start, stop, heads),
            [((rows * (stop - start), qkv_cols), bf), ((1, qkv_cols), fl)],
            [scal, cot, context, dense_w, turned, probs, *tables],
            [pltpu.VMEM((rows * (stop - start), qkv_cols), fl), pltpu.VMEM((rows * (stop - start), wide), bf)],
        )
        halves.append(half)
        grads.append(part)
    *norms, five = call(
        functools.partial(norm_back_body, m),
        [((rows, width), bf)] * m + [((8, width), fl)],
        [scal, *x_slots, cot, *halves, qkv_w, slope, inner_w, vec],
    )
    rest_keep, rest_send = call(
        functools.partial(rest_body, strip),
        [((4, strip, qkv_cols), bf)] * 2,
        [scal, first, *halves],
        [pltpu.VMEM((tokens, qkv_cols), bf)],
    )
    fives = [five] + [depth_swap(five, k) for k in range(1, m)]
    small_rows = -(-(8 + 4 * heads) // 16) * 16
    small_keep, small_send = call(
        functools.partial(small_body, (strip, heads)),
        [((4, small_rows, strip), bf)] * 2,
        [scal, *grads, inner_grad, *fives],
        [pltpu.VMEM((8, width), fl)],
    )
    arrived = depth_scatter(norms)
    rest = scatter_sum(rest_keep, rest_send)
    small = scatter_sum(small_keep, small_send)
    (result,) = call(
        functools.partial(result_body, len(mixed)), [((rows, width), bf)], [scal, x_own, vec, *mixed], final=True
    )
    s_inner, s_outer, s_dense = call(
        functools.partial(unpack_big_body, units, wide),
        [((strip, units), fl), ((units, strip), fl), ((wide, strip), fl)],
        [scal, *big],
        final=True,
    )
    (s_qkv,) = call(unpack_rest_body, [((strip, qkv_cols), fl)], [scal, *rest], final=True)
    s_qkv_b, s_inner_b, *five = call(
        functools.partial(unpack_small_body, (strip, heads, lanes)),
        [(qkv_bias.shape, fl), (inner_bias.shape, fl)] + [((lanes,), fl)] * 5,
        [scal, *small],
        final=True,
    )
    (in_grad,) = call(
        functools.partial(finish_body, len(arrived)), [((rows, width), bf)], [scal, x_own, g_own, *arrived], final=True
    )
    return (
        result[None],
        in_grad[None],
        s_qkv,
        s_qkv_b,
        s_dense,
        five[0],
        s_inner,
        s_inner_b,
        s_outer,
        five[0],
        five[1],
        five[2],
        five[3],
        five[4],
    )


def solution(mesh):
    n, m = mesh.shape[FSDP], mesh.shape[TENSOR]
    paired = n == 8 and m == 4
    shards = plain_shards
    if paired:

        def shards(*args):
            return pair_shards(*args)

    placed = (
        P(None, (FSDP, TENSOR), None),
        P(None, (FSDP, TENSOR), None),
        P(None, FSDP, None),
        P(None, FSDP, None),
        P(FSDP, TENSOR),
        P(TENSOR, FSDP),
        P(TENSOR, FSDP),
        P((FSDP, TENSOR)),
        P(FSDP, TENSOR),
        P(TENSOR, FSDP),
        P(TENSOR, FSDP),
        P((FSDP, TENSOR)),
        P((FSDP, TENSOR)),
        P((FSDP, TENSOR)),
        P((FSDP, TENSOR)),
        P((FSDP, TENSOR)),
    )
    return jax.shard_map(
        shards,
        mesh=mesh,
        in_specs=placed,
        out_specs=(
            P(None, (FSDP, TENSOR), None),
            P(None, (FSDP, TENSOR), None),
            P(FSDP, TENSOR),
            P(TENSOR, FSDP),
            P(TENSOR, FSDP),
            P((FSDP, TENSOR)),
            P(FSDP, TENSOR),
            P(TENSOR, FSDP),
            P(TENSOR, FSDP),
            P((FSDP, TENSOR)),
            P((FSDP, TENSOR)),
            P((FSDP, TENSOR)),
            P((FSDP, TENSOR)),
            P((FSDP, TENSOR)),
        ),
        check_vma=False,
    )
```
